256 devices in a mesh: dp: 4 (over x), label: 64 (over z, y, core).
Axes of the slice: x: 4, y: 4, z: 8, core: 2. Of those that a mesh axis runs over, the one named last changes fastest.
Arguments:
- encoded: bfloat16 [65536, 768], P(('dp', 'label')), may hold values from -8 to 8
- coarse_weight: bfloat16 [4096, 768], P(('dp', 'label')), may hold values from -1 to 1
- fine_weight: bfloat16 [4096, 128, 768], P(('dp', 'label')), may hold values from -0.21875 to 0.21875
- cluster_group: int32 [65536, 8], P(('dp', 'label')), may hold values from 0 to 255, all different within a row; in each aligned block of 256 rows (0 to 255, 256 to 511, ...) at most 12 rows name the same one
- cluster_member: int32 [65536, 8], P(('dp', 'label')), may hold values from 0 to 15
- positive: int32 [65536], P(('dp', 'label')), may hold values from 0 to 127
Outputs:
- row_loss: float32 [65536], P(('dp', 'label'))
- d_encoded: bfloat16 [65536, 768], P(('dp', 'label'))
- d_fine: bfloat16 [4096, 128, 768], P(('dp', 'label'))
- cluster_loss: float32 [4096], P(('dp', 'label'))
The draws below stay inside these ranges and needn't reach their ends.
Inputs may be any that keep to these rules, and one draw needn't show every extreme that they name: `cluster_group`: each row names 8 different groups. Among the rows of one device (aligned blocks of 256 rows) no group is named by more than 12 rows, a bound that some block reaches.
All inputs are finite; a program needn't handle non-finite values.
Results may differ from the reference program's by a relative error of at most 0.0051.
Values may be sent and summed in bfloat16 or wider, within the bound.
No kernel may reach another device: no remote copies, remote signals or barrier semaphores. Data moves between devices by JAX's collectives and lax.ppermute only.
A program may use at most 128 MiB of HBM per device.

```python
import math
import jax
import jax.numpy as jnp
import numpy as np
from jax import lax

D = 768
LBL = 128
TOP = 8
CL_DEV = 16
ROW_DEV = 256
ROWS = 65536
CLUSTERS = 4096
CAP = 12
N_DP = 4
N_LABEL = 64


def draw_encoded(key, part):
    drawn = jax.random.normal(jax.random.fold_in(key, 11), (ROWS, D), jnp.float32)
    return jnp.clip(drawn, -8.0, 8.0).astype(jnp.bfloat16)


def draw_coarse_weight(key, part):
    drawn = jax.random.normal(jax.random.fold_in(key, 21), (CLUSTERS, D), jnp.float32) / math.sqrt(D)
    scales = jnp.exp(jax.random.uniform(jax.random.fold_in(key, 22), (CLUSTERS, 1), jnp.float32, math.log(0.3), math.log(3.0)))
    weight = drawn * scales
    return jnp.clip(weight, -1.0, 1.0).astype(jnp.bfloat16)


def touch_ends(drawn, own_key, low, high):
    place = [jax.random.randint(jax.random.fold_in(own_key, axis), (), 0, length) for axis, length in enumerate(drawn.shape)]
    widest = drawn.shape.index(max(drawn.shape))
    next_to = place[:widest] + [(place[widest] + 1) % drawn.shape[widest]] + place[widest + 1:]
    return drawn.at[tuple(place)].set(low).at[tuple(next_to)].set(high)


def block_scale(own_key, extent, cuts, low, high):
    def one(dim, shards_of):
        draws = jax.random.uniform(jax.random.fold_in(jax.random.fold_in(own_key, 6), dim), (shards_of,), jnp.float32, low / len(cuts), high / len(cuts))
        return jnp.repeat(jnp.exp(draws), extent[dim] // shards_of).reshape((-1,) + (1,) * (len(extent) - dim - 1))

    loudness = one(*cuts[0])
    for cut in cuts[1:]:
        loudness = loudness * one(*cut)
    return loudness


def assign_block(own_key, own, number, rows, amount, top, most, skew):
    ranking = jax.random.permutation(own_key, amount)
    crowded, usual = portions_of(amount, rows * top, most, skew, True), portions_of(amount, rows * top, most, skew, False)
    places = jnp.arange(amount)

    def named(tallies, offset_by):
        used = int((tallies > 0).sum())
        fixed = max(1, used // 4)
        shifted = fixed + (places - fixed + offset_by * (used - fixed)) % max(1, amount - fixed)
        return jnp.zeros((amount,), jnp.int32).at[ranking[jnp.where(places < fixed, places, shifted)]].set(jnp.asarray(tallies, jnp.int32))

    tallies = jnp.where(number % 4 == 0, named(crowded, number // 4), named(usual, number - number // 4 - 1))
    mixed = jax.random.permutation(jax.random.fold_in(own, 3), amount)
    source_of, receiver = mixed[0:amount // 2 * 2:2], mixed[1:amount // 2 * 2:2]
    margin = jnp.minimum(tallies[source_of] - 1, most - tallies[receiver]) // 2
    margin = jnp.where((source_of == ranking[0]) | (receiver == ranking[0]) | (tallies[receiver] == 0), 0, jnp.maximum(margin, 0))
    shifted = jax.random.randint(jax.random.fold_in(own, 4), (amount // 2,), 0, 1 << 20) % (margin + 1)
    tallies = tallies.at[source_of].add(-shifted).at[receiver].add(shifted)
    labels = jnp.searchsorted(jnp.cumsum(tallies), jnp.arange(rows * top), side="right").astype(jnp.int32)
    listing = labels.reshape(top, rows).T
    listing = listing[jax.random.permutation(jax.random.fold_in(own, 1), rows)]
    offset_by = jax.random.randint(jax.random.fold_in(own, 2), (rows, 1), 0, top)
    return jnp.take_along_axis(listing, (jnp.arange(top)[None, :] + offset_by) % top, axis=1)


def portions_of(count, total, reach, lean, full):
    weights = [(1 << 20) // math.isqrt(grade ** lean) + 1 for grade in range(1, count + 1)]
    largest = reach if full else min(reach, max(-(-total // count), total * weights[0] // sum(weights)))
    least = 1 if total - largest >= count - 1 else 0
    holding, spare = [largest] + [least] * (count - 1), total - largest - least * (count - 1)
    while spare > 0:
        free = [i for i in range(1, count) if holding[i] < largest] or [i for i in range(1, count) if holding[i] < reach]
        mass, remaining = sum([weights[i] for i in free]), spare
        for i in free:
            more = min(reach - holding[i], max(1, remaining * weights[i] // mass), spare)
            holding[i] = holding[i] + more
            spare = spare - more
    return np.array(holding)


def normal_values(rng, dims, spread, reach, split=(), kind=jnp.bfloat16):
    entries = spread * jax.random.normal(rng, dims, jnp.float32)
    if split:
        entries = entries * block_scale(rng, dims, split, -0.22, 0.18)
    return jnp.clip(entries, -reach, reach).astype(kind)


def setup_inputs(seed: int = 0) -> dict:
    key_list = jax.random.split(jax.random.key(seed), 7)
    encoded = draw_encoded(jax.random.fold_in(key_list[6], 71), 0)
    coarse_weight = draw_coarse_weight(jax.random.fold_in(key_list[6], 71), 0)
    fine_weight = normal_values(key_list[2], (CLUSTERS, LBL, D), D ** -0.5, 0.21875, ((0, 256),))
    cluster_group_keys = jax.random.split(jax.random.fold_in(key_list[3], 1), ROWS // ROW_DEV)
    cluster_group_turns = jax.random.permutation(jax.random.fold_in(key_list[3], 3), ROWS // ROW_DEV)
    cluster_group = jax.vmap(lambda own, number: assign_block(jax.random.fold_in(key_list[3], 2), own, number, ROW_DEV, N_DP * N_LABEL, TOP, CAP, 2))(cluster_group_keys, cluster_group_turns).reshape((ROWS, TOP))
    cluster_member = touch_ends(jax.random.randint(key_list[4], (ROWS, TOP), 0, CL_DEV), jax.random.fold_in(key_list[4], 1), 0, CL_DEV - 1).astype(jnp.int32)
    positive = touch_ends(jax.random.randint(key_list[5], (ROWS,), 0, LBL), jax.random.fold_in(key_list[5], 1), 0, LBL - 1).astype(jnp.int32)
    return dict(encoded=encoded, coarse_weight=coarse_weight, fine_weight=fine_weight, cluster_group=cluster_group, cluster_member=cluster_member, positive=positive)


def softplus_loss(logits, truth):
    return jnp.maximum(logits, 0.0) + jnp.log1p(jnp.exp(-jnp.abs(logits))) - truth * logits


def reference(encoded, coarse_weight, fine_weight, cluster_group, cluster_member, positive):
    cluster = cluster_group * CL_DEV + cluster_member
    target = cluster[:, 0]
    row_total = encoded.shape[0]
    block_rows = 256
    clusters_all = coarse_weight.shape[0]
    column_ids = jnp.arange(clusters_all, dtype=jnp.int32)

    def coarse_block(pieces):
        rows_block, target_block = pieces
        scores = jnp.dot(rows_block, coarse_weight.T, preferred_element_type=jnp.float32)
        top_score = jnp.max(scores, axis=1, keepdims=True)
        logsum = top_score[:, 0] + jnp.log(jnp.sum(jnp.exp(scores - top_score), axis=1))
        is_target = column_ids[None, :] == target_block[:, None]
        target_score = jnp.sum(jnp.where(is_target, scores, 0.0), axis=1)
        grad_block = (jnp.exp(scores - logsum[:, None]) - is_target.astype(jnp.float32)).astype(jnp.bfloat16)
        back_block = jnp.dot(grad_block, coarse_weight, preferred_element_type=jnp.float32)
        return logsum - target_score, back_block

    row_loss, coarse_back = lax.map(coarse_block, (encoded.reshape(-1, block_rows, D), target.reshape(-1, block_rows)))
    row_loss = row_loss.reshape(row_total)
    coarse_back = coarse_back.reshape(row_total, D)

    slot_total = row_total * TOP
    keys = cluster.reshape(-1).astype(jnp.int32)
    sorted_index = jnp.argsort(keys, stable=True).astype(jnp.int32)
    counts = jax.ops.segment_sum(jnp.ones(slot_total, jnp.int32), keys, num_segments=clusters_all)
    starts = jnp.cumsum(counts) - counts
    window = 64
    padded = jnp.concatenate([sorted_index, jnp.zeros(window, jnp.int32)])
    label_ids = jnp.arange(LBL, dtype=jnp.int32)

    def per_cluster(back_rows, cluster_id):
        weight_now = lax.dynamic_index_in_dim(fine_weight, cluster_id, 0, keepdims=False)
        count_now = counts[cluster_id]
        start_now = starts[cluster_id]

        def per_window(block_index, carry):
            back_acc, weight_grad, loss_now = carry
            offset = block_index * window
            slot_ids = lax.dynamic_slice_in_dim(padded, (start_now + offset).astype(jnp.int32), window)
            usable = (offset + jnp.arange(window, dtype=jnp.int32)) < count_now
            row_ids = slot_ids // TOP
            in_row = slot_ids % TOP
            rows_now = encoded[row_ids]
            logits = jnp.dot(rows_now, weight_now.T, preferred_element_type=jnp.float32)
            truth = ((in_row == 0)[:, None] & (positive[row_ids][:, None] == label_ids[None, :])).astype(jnp.float32)
            mask = usable[:, None].astype(jnp.float32)
            loss_now = loss_now + jnp.sum(softplus_loss(logits, truth) * mask) / (TOP * LBL)
            grad_now = ((jax.nn.sigmoid(logits) - truth) / TOP * mask).astype(jnp.bfloat16)
            back_now = jnp.dot(grad_now, weight_now, preferred_element_type=jnp.float32).astype(jnp.bfloat16)
            back_acc = back_acc.at[row_ids].add(back_now.astype(jnp.float32))
            weight_grad = weight_grad + lax.dot_general(grad_now, rows_now, (((0,), (0,)), ((), ())), preferred_element_type=jnp.float32)
            return back_acc, weight_grad, loss_now

        blocks_now = (count_now + window - 1) // window
        start_carry = (back_rows, jnp.zeros((LBL, D), jnp.float32), jnp.zeros((), jnp.float32))
        back_rows, weight_grad, loss_now = lax.fori_loop(0, blocks_now, per_window, start_carry)
        return back_rows, (weight_grad.astype(jnp.bfloat16), loss_now)

    fine_back, outputs = lax.scan(per_cluster, jnp.zeros((row_total, D), jnp.float32), jnp.arange(clusters_all, dtype=jnp.int32))
    d_fine, cluster_loss = outputs
    d_encoded = (coarse_back + fine_back).astype(jnp.bfloat16)
    return row_loss, d_encoded, d_fine, cluster_loss
```

```python
import jax
import jax.numpy as jnp
from jax import lax
from jax.experimental import pallas as pl
from jax.experimental.pallas import tpu as pltpu
from jax.sharding import Mesh, PartitionSpec as P

CAP = 12
PAIR = 2 * CAP
PLANE = ("x", "y", "c")
EVERY = ("x", "z", "y", "c")
F32 = jnp.float32
BF16 = jnp.bfloat16
VMEM = pl.BlockSpec(memory_space=pltpu.VMEM)
NT = (((1,), (1,)), ((), ()))
TN = (((0,), (0,)), ((), ()))


def call(kernel, out_shape, args, flops, bytes_accessed, name):
    many = isinstance(out_shape, (list, tuple))
    return pl.pallas_call(
        kernel,
        out_shape=out_shape,
        in_specs=[VMEM] * len(args),
        out_specs=[VMEM] * len(out_shape) if many else VMEM,
        compiler_params=pltpu.CompilerParams(vmem_limit_bytes=40 * 2**20),
        cost_estimate=pl.CostEstimate(
            flops=flops, bytes_accessed=bytes_accessed, transcendentals=0
        ),
        name=name,
    )(*args)


def sds(shape, dtype):
    return jax.ShapeDtypeStruct(shape, dtype)


def plan_kernel(gid_ref, *refs):
    metas, (key_ref, code_ref) = refs[:8], refs[8:]
    dests = gid_ref.shape[0]
    rows = metas[0].shape[1]
    gid = jnp.broadcast_to(gid_ref[:, :1], (dests, rows))
    upper = (
        lax.broadcasted_iota(jnp.int32, (rows, rows), 0)
        < lax.broadcasted_iota(jnp.int32, (rows, rows), 1)
    ).astype(F32).astype(BF16)
    lanes = lax.broadcasted_iota(jnp.int32, (dests, 128), 1)
    code_ref[...] = jnp.zeros(code_ref.shape, code_ref.dtype)
    for chunk in range(4):
        codes = jnp.zeros((dests, 128), F32)
        for half in range(2):
            packed = metas[2 * chunk + half][...]
            group = packed >> 12
            load = (packed & 4095) + 1
            val = jnp.zeros((dests, rows), jnp.int32)
            for s in range(packed.shape[0]):
                val = val + jnp.where(group[s : s + 1, :] == gid, load[s : s + 1, :], 0)
            hit = (val > 0).astype(F32)
            rank = jnp.dot(hit.astype(BF16), upper, preferred_element_type=F32).astype(jnp.int32)
            key = jnp.where(val > 0, rank + half * CAP, -1)
            key_ref[chunk, :, half * rows : (half + 1) * rows] = key
            valf = val.astype(F32)
            for k in range(CAP):
                at = half * CAP + k
                found = jnp.sum(jnp.where(key == at, valf, 0.0), axis=1, keepdims=True)
                codes = jnp.where(lanes == at, found, codes)
        code_ref[:, chunk, :] = codes.astype(jnp.int32)


def one_hot(key):
    dests, rows = key.shape
    at = lax.broadcasted_iota(jnp.int32, (dests, PAIR, rows), 1)
    hot = jnp.where(jnp.broadcast_to(key[:, None, :], at.shape) == at, 1.0, 0.0)
    return hot.reshape(dests * PAIR, rows).astype(BF16)


def pack_kernel(chunk, key_ref, *refs):
    rows_refs, out_ref = refs[:-1], refs[-1]
    hot = one_hot(key_ref[chunk])
    start, total = 0, None
    for r in rows_refs:
        part = jnp.dot(hot[:, start : start + r.shape[0]], r[...], preferred_element_type=F32)
        total = part if total is None else total + part
        start += r.shape[0]
    out_ref[...] = total.astype(BF16)


def unpack_kernel(chunk, key_ref, back_ref, a_ref, b_ref):
    hot = one_hot(key_ref[chunk])
    half = a_ref.shape[0]
    total = lax.dot_general(hot, back_ref[...], TN, preferred_element_type=F32)
    a_ref[...] = total[:half]
    b_ref[...] = total[half:]


def fine_kernel(chunk, per_row, code_ref, rows_ref, w_ref, grad_ref, mem_ref, back_ref, loss_ref):
    dests = code_ref.shape[0]
    slots = dests * PAIR
    clusters, labels, features = w_ref.shape
    w = w_ref[...].reshape(clusters * labels, features)
    codes = code_ref[:, chunk, :].astype(F32)
    lane = lax.broadcasted_iota(jnp.int32, (dests, PAIR, 128), 2)
    at = lax.broadcasted_iota(jnp.int32, (dests, PAIR, 128), 1)
    spread = jnp.where(lane == at, jnp.broadcast_to(codes[:, None, :], lane.shape), 0.0)
    code = jnp.sum(spread, axis=2, keepdims=True).reshape(slots, 1).astype(jnp.int32)
    step = 256
    losses = jnp.zeros((1, 128), F32)
    for t in range(slots // step):
        here = slice(t * step, (t + 1) * step)
        mine = code[here]
        member = jnp.where(mine > 0, (mine - 1) >> 8, clusters)
        truth_id = (mine - 1) & 255
        all_logits = lax.dot_general(rows_ref[here, :], w, NT, preferred_element_type=F32)
        member_l = jnp.broadcast_to(member, (step, labels))
        logits = jnp.zeros((step, labels), F32)
        for m in range(clusters):
            logits = jnp.where(member_l == m, all_logits[:, m * labels : (m + 1) * labels], logits)
        label = lax.broadcasted_iota(jnp.int32, (step, labels), 1)
        truth = jnp.where(label == jnp.broadcast_to(truth_id, (step, labels)), 1.0, 0.0)
        bce = jnp.maximum(logits, 0.0) + jnp.log1p(jnp.exp(-jnp.abs(logits))) - truth * logits
        row_loss = jnp.sum(bce, axis=1, keepdims=True) / (per_row * labels)
        losses = losses + jnp.sum(
            jnp.where(label == member_l, jnp.broadcast_to(row_loss, (step, labels)), 0.0),
            axis=0,
            keepdims=True,
        )
        grad = ((jax.nn.sigmoid(logits) - truth) / per_row).astype(BF16).astype(F32)
        wide = jnp.concatenate(
            [jnp.where(member_l == m, grad, 0.0).astype(BF16) for m in range(clusters)], axis=1
        )
        back_ref[here, :] = jnp.dot(wide, w, preferred_element_type=F32).astype(BF16)
        grad_ref[:, here] = grad.T.astype(BF16)
        mem_ref[:, here] = member_l.astype(F32).T[:8].astype(jnp.int32)
    loss_ref[...] = jnp.broadcast_to(losses, loss_ref.shape)


def weight_kernel(*refs):
    grads, mems, rows, out_ref = refs[:4], refs[4:8], refs[8:12], refs[12]
    each, labels, features = out_ref.shape
    first = pl.program_id(0) * each
    total = None
    for g_ref, m_ref, r_ref in zip(grads, mems, rows):
        grad = g_ref[...].astype(F32)
        mem = jnp.broadcast_to(m_ref[:1, :], grad.shape)
        wide = jnp.concatenate(
            [jnp.where(mem == first + m, grad, 0.0).astype(BF16) for m in range(each)], axis=0
        )
        part = jnp.dot(wide, r_ref[...], preferred_element_type=F32)
        total = part if total is None else total + part
    out_ref[...] = total.astype(BF16).reshape(out_ref.shape)


def coarse_kernel(target_ref, rows_ref, w_ref, loss_ref, back_ref):
    w = w_ref[...]
    scores = lax.dot_general(rows_ref[...], w, NT, preferred_element_type=F32)
    column = lax.broadcasted_iota(jnp.int32, scores.shape, 1)
    is_target = column == jnp.broadcast_to(target_ref[:, :1], scores.shape)
    top = jnp.max(scores, axis=1, keepdims=True)
    lifted = jnp.exp(scores - top)
    total = jnp.sum(lifted, axis=1, keepdims=True)
    at_target = jnp.sum(jnp.where(is_target, scores, 0.0), axis=1, keepdims=True)
    grad = (lifted * (1.0 / total) - jnp.where(is_target, 1.0, 0.0)).astype(BF16)
    back_ref[...] = jnp.dot(grad, w, preferred_element_type=F32)
    loss_ref[...] = jnp.broadcast_to(top + jnp.log(total) - at_target, loss_ref.shape)


def coarse_part(target, rows, weight):
    own, features = rows.shape
    tile = 128
    return pl.pallas_call(
        coarse_kernel,
        grid=(own // tile,),
        out_shape=[sds((own, 128), F32), sds((own, features), F32)],
        in_specs=[
            pl.BlockSpec((tile, 128), lambda i: (i, 0)),
            pl.BlockSpec((tile, features), lambda i: (i, 0)),
            pl.BlockSpec(weight.shape, lambda i: (0, 0), pipeline_mode=pl.Buffered(1)),
        ],
        out_specs=[
            pl.BlockSpec((tile, 128), lambda i: (i, 0)),
            pl.BlockSpec((tile, features), lambda i: (i, 0)),
        ],
        compiler_params=pltpu.CompilerParams(vmem_limit_bytes=40 * 2**20),
        cost_estimate=pl.CostEstimate(
            flops=4 * own * features * weight.shape[0],
            bytes_accessed=10 * 2**20,
            transcendentals=own * weight.shape[0],
        ),
        name="coarse",
    )(jnp.broadcast_to(target[:, None], (own, 128)), rows, weight)


def weight_part(grads, mems, rows, shape):
    clusters, labels, features = shape
    each = 4
    const = lambda a: pl.BlockSpec(a.shape, lambda i: (0, 0), pipeline_mode=pl.Buffered(1))
    args = (*grads, *mems, *rows)
    return pl.pallas_call(
        weight_kernel,
        grid=(clusters // each,),
        out_shape=sds(shape, BF16),
        in_specs=[const(a) for a in args],
        out_specs=pl.BlockSpec((each, labels, features), lambda i: (i, 0, 0)),
        compiler_params=pltpu.CompilerParams(vmem_limit_bytes=40 * 2**20),
        cost_estimate=pl.CostEstimate(
            flops=2 * clusters * labels * features * 3072, bytes_accessed=9 * 2**20, transcendentals=0
        ),
        name="weights",
    )(*args)


def per_device(encoded, coarse_weight, fine_weight, cluster_group, cluster_member, positive):
    own, features = encoded.shape
    clusters, labels, _ = fine_weight.shape
    per_row = cluster_group.shape[1]
    n_z = lax.axis_size("z")
    plane = lax.axis_size(PLANE)
    each_row = lax.axis_size("y") * lax.axis_size("c")
    z = lax.axis_index("z")
    ring = {d: [(i, (i + d) % n_z) for i in range(n_z)] for d in range(-4, 5)}

    def shift(value, by):
        return lax.ppermute(value, "z", ring[by])

    full_weight = lax.all_gather(coarse_weight, EVERY, axis=0, tiled=True)

    label = jnp.where(jnp.arange(per_row)[None, :] == 0, positive[:, None], 255)
    meta = ((cluster_group << 12) + (cluster_member << 8) + label).T
    order = (0, -1, 1, -2, 2, -3, 3, 4)
    metas = [meta if o == 0 else shift(meta, -o) for o in order]
    dest = jnp.arange(plane, dtype=jnp.int32)
    gid = (dest // each_row) * (each_row * n_z) + z * each_row + dest % each_row
    gid = jnp.broadcast_to(gid[:, None], (plane, 128))
    slots = plane * PAIR
    key, code = call(
        plan_kernel,
        [sds((4, plane, 2 * own), jnp.int32), sds((plane, 8, 128), jnp.int32)],
        (gid, *metas),
        2 * 8 * plane * own * own,
        10**6,
        "plan",
    )
    code_in = lax.all_to_all(code, PLANE, 0, 0, tiled=True)

    up, down = [encoded], [encoded]
    for step in range(3):
        up.append(shift(up[-1], 1))
        down.append(shift(down[-1], -1))
    half = own // 2
    far_up, far_down = shift(up[3][:half], 1), shift(down[3][half:], -1)
    held = [(encoded, up[1]), (down[1], up[2]), (down[2], up[3]), (down[3], far_up, far_down)]
    rows_in = []
    for chunk in range(4):
        packed = call(
            lambda *r, chunk=chunk: pack_kernel(chunk, *r),
            sds((slots, features), BF16),
            (key, *held[chunk]),
            2 * slots * 2 * own * features,
            3 * 10**6,
            f"pack{chunk}",
        )
        moved = lax.all_to_all(packed.reshape(plane, PAIR, features), PLANE, 0, 0, tiled=True)
        rows_in.append(moved.reshape(slots, features))

    fine = []
    for chunk in range(4):
        fine.append(
            call(
                lambda *r, chunk=chunk: fine_kernel(chunk, per_row, *r),
                [
                    sds((labels, slots), BF16),
                    sds((8, slots), jnp.int32),
                    sds((slots, features), BF16),
                    sds((8, 128), F32),
                ],
                (code_in, rows_in[chunk], fine_weight),
                4 * slots * clusters * labels * features,
                7 * 10**6,
                f"fine{chunk}",
            )
        )
    cluster_loss = sum(f[3] for f in fine)[0, :clusters]

    part = {}
    for chunk in (3, 2, 1, 0):
        back = lax.all_to_all(
            fine[chunk][2].reshape(plane, PAIR, features), PLANE, 0, 0, tiled=True
        ).reshape(slots, features)
        part[order[2 * chunk]], part[order[2 * chunk + 1]] = call(
            lambda *r, chunk=chunk: unpack_kernel(chunk, *r),
            [sds((own, features), F32)] * 2,
            (key, back),
            2 * slots * 2 * own * features,
            4 * 10**6,
            f"unpack{chunk}",
        )
    d_fine = weight_part([f[0] for f in fine], [f[1] for f in fine], rows_in, fine_weight.shape)
    row_loss, coarse_back = coarse_part(
        cluster_group[:, 0] * clusters + cluster_member[:, 0], encoded, full_weight
    )

    far = part[4].astype(BF16)
    got_down, got_up = shift(far[:half], -1), shift(far[half:], 1)
    go_down = part[-3] + jnp.pad(got_down.astype(F32), ((0, half), (0, 0)))
    go_up = part[3] + jnp.pad(got_up.astype(F32), ((half, 0), (0, 0)))
    for o in (2, 1, 0):
        got_down = shift(go_down.astype(BF16), -1).astype(F32)
        got_up = shift(go_up.astype(BF16), 1).astype(F32)
        if o:
            go_down, go_up = part[-o] + got_down, part[o] + got_up
    d_encoded = (coarse_back + part[0] + got_down + got_up).astype(BF16)
    return row_loss[:, 0], d_encoded, d_fine, cluster_loss


def solution(mesh):
    fine_mesh = Mesh(mesh.devices.reshape(4, 8, 4, 2), EVERY)
    rows = P(EVERY)
    wide = P(EVERY, None)
    cube = P(EVERY, None, None)
    return jax.shard_map(
        per_device,
        mesh=fine_mesh,
        in_specs=(wide, wide, cube, wide, wide, rows),
        out_specs=(rows, wide, cube, rows),
        check_vma=False,
    )
```

```python
import jax
import jax.numpy as jnp
from jax import lax
from jax.experimental import pallas as pl
from jax.experimental.pallas import tpu as pltpu
from jax.sharding import Mesh, PartitionSpec as P

CAP = 12
EMPTY = 128
PLANE = ("x", "y", "c")
EVERY = ("x", "z", "y", "c")
F32 = jnp.float32
BF16 = jnp.bfloat16
VMEM = pl.BlockSpec(memory_space=pltpu.VMEM)
NT = (((1,), (1,)), ((), ()))
TN = (((0,), (0,)), ((), ()))


def call(kernel, out_shape, args, flops, bytes_accessed, name):
    many = isinstance(out_shape, (list, tuple))
    return pl.pallas_call(
        kernel,
        out_shape=out_shape,
        in_specs=[VMEM] * len(args),
        out_specs=[VMEM] * len(out_shape) if many else VMEM,
        compiler_params=pltpu.CompilerParams(vmem_limit_bytes=40 * 2**20),
        cost_estimate=pl.CostEstimate(
            flops=flops, bytes_accessed=bytes_accessed, transcendentals=0
        ),
        name=name,
    )(*args)


def sds(shape, dtype):
    return jax.ShapeDtypeStruct(shape, dtype)


def plan(meta, gid, upper):
    dests, rows = gid.shape
    group, member, label = meta[:, :rows], meta[:, rows : 2 * rows], meta[:, 2 * rows :]
    load = member * 256.0 + label + 1.0
    val = jnp.zeros((dests, rows), F32)
    for s in range(meta.shape[0]):
        val = val + jnp.where(group[s : s + 1, :] == gid, load[s : s + 1, :], 0.0)
    hit = jnp.where(val > 0.0, 1.0, 0.0).astype(BF16)
    rank = jnp.dot(hit, upper, preferred_element_type=F32)
    return val, jnp.where(val > 0.0, rank, -1.0).astype(jnp.int32)


def one_hot(key, each):
    dests, rows = key.shape
    at = lax.broadcasted_iota(jnp.int32, (dests, each, rows), 1)
    hot = jnp.where(jnp.broadcast_to(key[:, None, :], at.shape) == at, 1.0, 0.0)
    return hot.reshape(dests * each, rows).astype(BF16)


def pack_kernel(pieces, each, gid_ref, *refs):
    rows_refs, (out_ref, key_ref) = refs[:-2], refs[-2:]
    _, dests, rows = key_ref.shape
    gid = jnp.broadcast_to(gid_ref[:, :1], (dests, rows))
    upper = jnp.where(
        lax.broadcasted_iota(jnp.int32, (rows, rows), 0)
        < lax.broadcasted_iota(jnp.int32, (rows, rows), 1),
        1.0,
        0.0,
    ).astype(BF16)
    lanes = lax.broadcasted_iota(jnp.int32, (dests, 128), 1)
    codes = jnp.zeros((dests, 128), F32)
    total, first = None, 0
    for i, count in enumerate(pieces):
        mine = rows_refs[first : first + count]
        first += count
        size = mine[-1].shape[0]
        val, slot = plan(mine[-1][size - 8 :, :].astype(F32), gid, upper)
        for k in range(CAP):
            found = jnp.sum(jnp.where(slot == k, val, 0.0), axis=1, keepdims=True)
            codes = jnp.where(lanes == i * CAP + k, found, codes)
        key = jnp.where(slot >= 0, slot + i * CAP, -1)
        key_ref[i] = key
        hot = one_hot(key, each)
        start = 0
        for r in mine:
            count_rows = min(r.shape[0], rows - start)
            part = jnp.dot(
                hot[:, start : start + count_rows],
                r[:count_rows, :],
                preferred_element_type=F32,
            )
            total = part if total is None else total + part
            start += count_rows
    code = codes.astype(jnp.int32)
    member = jnp.where(code > 0, (code - 1) >> 8, EMPTY)
    label = jnp.where(code > 0, (code - 1) & 255, 255)
    used = len(pieces) * CAP
    at = lax.broadcasted_iota(jnp.int32, (dests, each, 128), 1)
    extra = jnp.where(
        at == used,
        jnp.broadcast_to(member.astype(F32)[:, None, :], at.shape),
        jnp.where(
            at == used + 1, jnp.broadcast_to(label.astype(F32)[:, None, :], at.shape), 0.0
        ),
    ).reshape(dests * each, 128)
    out_ref[:, :128] = (total[:, :128] + extra).astype(BF16)
    out_ref[:, 128:] = total[:, 128:].astype(BF16)


def unpack_kernel(each, key_ref, back_ref, *outs):
    for i, out in enumerate(outs):
        hot = one_hot(key_ref[i], each)
        out[...] = lax.dot_general(hot, back_ref[...], TN, preferred_element_type=F32)


def fine_kernel(each, used, per_row, rows_ref, w_ref, grad_ref, mem_ref, back_ref, loss_ref):
    slots = rows_ref.shape[0]
    dests = slots // each
    clusters, labels, features = w_ref.shape
    w = w_ref[...].reshape(clusters * labels, features)
    lane = lax.broadcasted_iota(jnp.int32, (dests, each, 128), 2)
    at = lax.broadcasted_iota(jnp.int32, (dests, each, 128), 1)
    lead = rows_ref[:, :128].astype(F32).reshape(dests, each, 128)

    def column(row):
        flat = jnp.sum(jnp.where(at == row, lead, 0.0), axis=1, keepdims=True)
        spread = jnp.where(lane == at, jnp.broadcast_to(flat, lead.shape), 0.0)
        return jnp.sum(spread, axis=2, keepdims=True).reshape(slots, 1).astype(jnp.int32)

    members, truths = column(used), column(used + 1)
    step = 256
    losses = jnp.zeros((1, 128), F32)
    for t in range(slots // step):
        here = slice(t * step, (t + 1) * step)
        all_logits = lax.dot_general(rows_ref[here, :], w, NT, preferred_element_type=F32)
        member_l = jnp.broadcast_to(members[here], (step, labels))
        logits = jnp.zeros((step, labels), F32)
        for m in range(clusters):
            logits = jnp.where(member_l == m, all_logits[:, m * labels : (m + 1) * labels], logits)
        label = lax.broadcasted_iota(jnp.int32, (step, labels), 1)
        truth = jnp.where(label == jnp.broadcast_to(truths[here], (step, labels)), 1.0, 0.0)
        bce = jnp.maximum(logits, 0.0) + jnp.log1p(jnp.exp(-jnp.abs(logits))) - truth * logits
        row_loss = jnp.sum(bce, axis=1, keepdims=True) / (per_row * labels)
        losses = losses + jnp.sum(
            jnp.where(label == member_l, jnp.broadcast_to(row_loss, (step, labels)), 0.0),
            axis=0,
            keepdims=True,
        )
        grad = ((jax.nn.sigmoid(logits) - truth) / per_row).astype(BF16).astype(F32)
        wide = jnp.concatenate(
            [jnp.where(member_l == m, grad, 0.0).astype(BF16) for m in range(clusters)], axis=1
        )
        back_ref[here, :] = jnp.dot(wide, w, preferred_element_type=F32).astype(BF16)
        grad_ref[:, here] = grad.T.astype(BF16)
        mem_ref[:, here] = member_l.astype(F32).T[:8].astype(jnp.int32)
    loss_ref[...] = jnp.broadcast_to(losses, loss_ref.shape)


def weight_kernel(*refs):
    grads, mems, rows, out_ref = refs[:2], refs[2:4], refs[4:6], refs[6]
    each, labels, features = out_ref.shape
    first = pl.program_id(0) * each
    total = None
    for g_ref, m_ref, r_ref in zip(grads, mems, rows):
        grad = g_ref[...].astype(F32)
        mem = jnp.broadcast_to(m_ref[:1, :], grad.shape)
        wide = jnp.concatenate(
            [jnp.where(mem == first + m, grad, 0.0).astype(BF16) for m in range(each)], axis=0
        )
        part = jnp.dot(wide, r_ref[...], preferred_element_type=F32)
        total = part if total is None else total + part
    out_ref[...] = total.astype(BF16).reshape(out_ref.shape)


def coarse_kernel(target_ref, rows_ref, w_ref, loss_ref, back_ref):
    w = w_ref[...]
    scores = lax.dot_general(rows_ref[...], w, NT, preferred_element_type=F32)
    column = lax.broadcasted_iota(jnp.int32, scores.shape, 1)
    is_target = column == jnp.broadcast_to(target_ref[:, :1], scores.shape)
    top = jnp.max(scores, axis=1, keepdims=True)
    lifted = jnp.exp(scores - top)
    total = jnp.sum(lifted, axis=1, keepdims=True)
    at_target = jnp.sum(jnp.where(is_target, scores, 0.0), axis=1, keepdims=True)
    grad = (lifted * (1.0 / total) - jnp.where(is_target, 1.0, 0.0)).astype(BF16)
    back_ref[...] = jnp.dot(grad, w, preferred_element_type=F32)
    loss_ref[...] = jnp.broadcast_to(top + jnp.log(total) - at_target, loss_ref.shape)


def coarse_part(target, rows, weight):
    own, features = rows.shape
    tile = 128
    return pl.pallas_call(
        coarse_kernel,
        grid=(own // tile,),
        out_shape=[sds((own, 128), F32), sds((own, features), F32)],
        in_specs=[
            pl.BlockSpec((tile, 128), lambda i: (i, 0)),
            pl.BlockSpec((tile, features), lambda i: (i, 0)),
            pl.BlockSpec(weight.shape, lambda i: (0, 0), pipeline_mode=pl.Buffered(1)),
        ],
        out_specs=[
            pl.BlockSpec((tile, 128), lambda i: (i, 0)),
            pl.BlockSpec((tile, features), lambda i: (i, 0)),
        ],
        compiler_params=pltpu.CompilerParams(vmem_limit_bytes=40 * 2**20),
        cost_estimate=pl.CostEstimate(
            flops=4 * own * features * weight.shape[0],
            bytes_accessed=10 * 2**20,
            transcendentals=own * weight.shape[0],
        ),
        name="coarse",
    )(jnp.broadcast_to(target[:, None], (own, 128)), rows, weight)


def weight_part(grads, mems, rows, shape):
    clusters, labels, features = shape
    each = 4
    const = lambda a: pl.BlockSpec(a.shape, lambda i: (0, 0), pipeline_mode=pl.Buffered(1))
    args = (*grads, *mems, *rows)
    return pl.pallas_call(
        weight_kernel,
        grid=(clusters // each,),
        out_shape=sds(shape, BF16),
        in_specs=[const(a) for a in args],
        out_specs=pl.BlockSpec((each, labels, features), lambda i: (i, 0, 0)),
        compiler_params=pltpu.CompilerParams(vmem_limit_bytes=40 * 2**20),
        cost_estimate=pl.CostEstimate(
            flops=2 * clusters * labels * features * rows[0].shape[0] * 3, bytes_accessed=9 * 2**20, transcendentals=0
        ),
        name="weights",
    )(*args)


def per_device(encoded, coarse_weight, fine_weight, cluster_group, cluster_member, positive):
    own, features = encoded.shape
    clusters, labels, _ = fine_weight.shape
    per_row = cluster_group.shape[1]
    n_z = lax.axis_size("z")
    plane = lax.axis_size(PLANE)
    each_row = lax.axis_size("y") * lax.axis_size("c")
    z = lax.axis_index("z")
    half = own // 2

    def shift(value, by):
        return lax.ppermute(value, "z", [(i, (i + by) % n_z) for i in range(n_z)])

    def exchange(value):
        slots = value.shape[0]
        cube = value.reshape(plane, slots // plane, features)
        return lax.all_to_all(cube, PLANE, 0, 0, tiled=True).reshape(slots, features)

    full_weight = lax.all_gather(coarse_weight, EVERY, axis=0, tiled=True)

    label = jnp.where(jnp.arange(per_row)[None, :] == 0, positive[:, None], 255)
    meta = jnp.concatenate([cluster_group, cluster_member, label], axis=0).astype(BF16).T
    source = jnp.concatenate([encoded, meta], axis=0)
    up, down = [source], [source]
    for step in range(3):
        up.append(shift(up[-1], 1))
        down.append(shift(down[-1], -1))
    far_up, far_down = shift(up[3][:half], 1), shift(down[3][half:], -1)

    dest = jnp.arange(plane, dtype=jnp.int32)
    gid = (dest // each_row) * (each_row * n_z) + z * each_row + dest % each_row
    gid = jnp.broadcast_to(gid[:, None], (plane, 128)).astype(F32)

    chunks = (
        ("near", (1, 1, 1), 40, (source, up[1], down[1])),
        ("far", (1, 1, 1, 1, 2), 64, (up[2], down[2], up[3], down[3], far_up, far_down)),
    )
    keys, rows_in, fine = [], [], []
    for name, pieces, each, held in chunks:
        slots = plane * each
        packed, key = call(
            lambda *r, pieces=pieces, each=each: pack_kernel(pieces, each, *r),
            [sds((slots, features), BF16), sds((len(pieces), plane, own), jnp.int32)],
            (gid, *held),
            2 * slots * len(pieces) * own * features,
            5 * 10**6,
            "pack_" + name,
        )
        keys.append(key)
        rows_in.append(exchange(packed))
        fine.append(
            call(
                lambda *r, pieces=pieces, each=each: fine_kernel(
                    each, len(pieces) * CAP, per_row, *r
                ),
                [
                    sds((labels, slots), BF16),
                    sds((8, slots), jnp.int32),
                    sds((slots, features), BF16),
                    sds((8, 128), F32),
                ],
                (rows_in[-1], fine_weight),
                4 * slots * clusters * labels * features,
                9 * 10**6,
                "fine_" + name,
            )
        )
    cluster_loss = (fine[0][3] + fine[1][3])[0, :clusters]

    def unpack(key, back, each, name):
        return call(
            lambda *r: unpack_kernel(each, *r),
            [sds((own, features), F32)] * key.shape[0],
            (key, back),
            2 * back.shape[0] * key.shape[0] * own * features,
            6 * 10**6,
            "unpack_" + name,
        )

    back_far = exchange(fine[1][2])
    back_near, back_far = lax.optimization_barrier((fine[0][2], back_far))
    back_near = exchange(back_near)
    at_m2, at_2, at_m3, at_3, at_4 = unpack(keys[1], back_far, 64, "far")
    d_fine = weight_part([f[0] for f in fine], [f[1] for f in fine], rows_in, fine_weight.shape)
    row_loss, coarse_back = coarse_part(
        cluster_group[:, 0] * clusters + cluster_member[:, 0], encoded, full_weight
    )

    far = at_4.astype(BF16)
    got_down, got_up = shift(far[:half], -1), shift(far[half:], 1)
    go_down = at_m3 + jnp.pad(got_down.astype(F32), ((0, half), (0, 0)))
    go_up = at_3 + jnp.pad(got_up.astype(F32), ((half, 0), (0, 0)))
    go_down = at_m2 + shift(go_down.astype(BF16), -1).astype(F32)
    go_up = at_2 + shift(go_up.astype(BF16), 1).astype(F32)
    got_down, got_up = shift(go_down.astype(BF16), -1), shift(go_up.astype(BF16), 1)
    back_near, coarse_back, got_down, got_up = lax.optimization_barrier(
        (back_near, coarse_back, got_down, got_up)
    )
    at_0, at_m1, at_1 = unpack(keys[0], back_near, 40, "near")
    got_down = shift((at_m1 + got_down.astype(F32)).astype(BF16), -1).astype(F32)
    got_up = shift((at_1 + got_up.astype(F32)).astype(BF16), 1).astype(F32)
    d_encoded = (coarse_back + at_0 + got_down + got_up).astype(BF16)
    return row_loss[:, 0], d_encoded, d_fine, cluster_loss


def solution(mesh):
    fine_mesh = Mesh(mesh.devices.reshape(4, 8, 4, 2), EVERY)
    rows = P(EVERY)
    wide = P(EVERY, None)
    cube = P(EVERY, None, None)
    return jax.shard_map(
        per_device,
        mesh=fine_mesh,
        in_specs=(wide, wide, cube, wide, wide, rows),
        out_specs=(rows, wide, cube, rows),
        check_vma=False,
    )
```

```python
import jax
import jax.numpy as jnp
from jax import lax
from jax.experimental import pallas as pl
from jax.experimental.pallas import tpu as pltpu
from jax.sharding import Mesh, PartitionSpec as P

CAP = 12
LIMIT = 56 * 2**20
PACKED = pl.CostEstimate(flops=10**11, bytes_accessed=6 * 10**6, transcendentals=0)
COST = pl.CostEstimate(flops=1, bytes_accessed=1, transcendentals=0)
EMPTY = 128
PLANE = ("x", "y", "c")
EVERY = ("x", "z", "y", "c")
F32 = jnp.float32
BF16 = jnp.bfloat16
NT = (((1,), (1,)), ((), ()))
TN = (((0,), (0,)), ((), ()))


def whole(a):
    return pl.BlockSpec(a.shape, lambda i: (0,) * len(a.shape), pipeline_mode=pl.Buffered(1))


def call(kernel, out_shape, args, name):
    return pl.pallas_call(
        kernel,
        grid=(1,),
        out_shape=out_shape,
        in_specs=[whole(a) for a in args],
        out_specs=[whole(o) for o in out_shape],
        compiler_params=pltpu.CompilerParams(vmem_limit_bytes=LIMIT),
        cost_estimate=PACKED if name.startswith("pack_far") else COST,
        name=name,
    )(*args)


def sds(shape, dtype):
    return jax.ShapeDtypeStruct(shape, dtype)


def plan(meta, gid, upper):
    dests, rows = gid.shape
    group, member, label = meta[:, :rows], meta[:, rows : 2 * rows], meta[:, 2 * rows :]
    load = member * 256.0 + label + 1.0
    val = jnp.zeros((dests, rows), F32)
    for s in range(meta.shape[0]):
        val = val + jnp.where(group[s : s + 1, :] == gid, load[s : s + 1, :], 0.0)
    hit = jnp.where(val > 0.0, 1.0, 0.0).astype(BF16)
    rank = jnp.dot(hit, upper, preferred_element_type=F32)
    return val, jnp.where(val > 0.0, rank, -1.0).astype(jnp.int32)


def one_hot(key, each):
    dests, rows = key.shape
    at = lax.broadcasted_iota(jnp.int32, (dests, each, rows), 1)
    hot = jnp.where(jnp.broadcast_to(key[:, None, :], at.shape) == at, 1.0, 0.0)
    return hot.reshape(dests * each, rows).astype(BF16)


def packed(pieces, each, lane0, used, gid_ref, rows_refs, key_ref):
    _, dests, rows = key_ref.shape
    gid = jnp.broadcast_to(gid_ref[:, :1], (dests, rows))
    upper = jnp.where(
        lax.broadcasted_iota(jnp.int32, (rows, rows), 0)
        < lax.broadcasted_iota(jnp.int32, (rows, rows), 1),
        1.0,
        0.0,
    ).astype(BF16)
    lanes = lax.broadcasted_iota(jnp.int32, (dests, 128), 1)
    codes = jnp.zeros((dests, 128), F32)
    total, first = None, 0
    for i, count in enumerate(pieces):
        mine = rows_refs[first : first + count]
        first += count
        size = mine[-1].shape[0]
        val, slot = plan(mine[-1][size - 8 :, :].astype(F32), gid, upper)
        for k in range(CAP):
            found = jnp.sum(jnp.where(slot == k, val, 0.0), axis=1, keepdims=True)
            codes = jnp.where(lanes == lane0 + i * CAP + k, found, codes)
        key = jnp.where(slot >= 0, slot + i * CAP, -1)
        key_ref[i] = key
        hot = one_hot(key, each)
        start = 0
        for r in mine:
            count_rows = min(r.shape[0], rows - start)
            part = jnp.dot(
                hot[:, start : start + count_rows],
                r[:count_rows, :],
                preferred_element_type=F32,
            )
            total = part if total is None else total + part
            start += count_rows
    code = codes.astype(jnp.int32)
    held = (lanes >= lane0) & (lanes < used)
    member = jnp.where(code > 0, (code - 1) >> 8, jnp.where(held, EMPTY, 0)).astype(F32)
    label = jnp.where(code > 0, (code - 1) & 255, 0).astype(F32)
    return total, member, label


def code_rows(member, label, each, row):
    dests = member.shape[0]
    at = lax.broadcasted_iota(jnp.int32, (dests, each, 128), 1)
    return jnp.where(
        at == row,
        jnp.broadcast_to(member[:, None, :], at.shape),
        jnp.where(at == row + 1, jnp.broadcast_to(label[:, None, :], at.shape), 0.0),
    ).reshape(dests * each, 128)


def pack_kernel(pieces, lane0, gid_ref, *refs):
    rows_refs, (out_ref, key_ref) = refs[:-2], refs[-2:]
    total, member, label = packed(pieces, 40, lane0, 128, gid_ref, rows_refs, key_ref)
    extra = code_rows(member, label, 40, 3 * CAP)
    out_ref[:, :128] = (total[:, :128] + extra).astype(BF16)
    out_ref[:, 128:] = total[:, 128:].astype(BF16)


def join_kernel(gid_ref, up_ref, down_ref, tail_ref, out_ref, key_ref):
    dests = gid_ref.shape[0]
    total, member, label = packed((1, 1), 24, 0, 24, gid_ref, (up_ref, down_ref), key_ref)
    extra = code_rows(member, label, 40, 3 * CAP)
    tail = tail_ref[...].astype(F32)
    for lo, hi in ((0, 128), (128, total.shape[1])):
        end = tail[:, lo:hi] + extra if lo == 0 else tail[:, lo:hi]
        both = jnp.concatenate(
            [total[:, lo:hi].reshape(dests, 24, hi - lo), end.reshape(dests, 40, hi - lo)], axis=1
        )
        out_ref[:, lo:hi] = both.reshape(dests * 64, hi - lo).astype(BF16)


def unpacked(key, back_ref, each):
    return lax.dot_general(one_hot(key, each), back_ref[...], TN, preferred_element_type=F32)


def unpack_far_kernel(offset, key_ref, back_ref, *outs):
    for i, out in enumerate(outs):
        key = jnp.where(key_ref[i] >= 0, key_ref[i] + offset, -1)
        out[...] = unpacked(key, back_ref, 64).astype(out.dtype)


def unpack_near_kernel(each, key_ref, back_ref, coarse_ref, down_ref, up_ref, own_out, down_out, up_out):
    down_out[...] = (unpacked(key_ref[1], back_ref, each) + down_ref[...].astype(F32)).astype(BF16)
    up_out[...] = (unpacked(key_ref[2], back_ref, each) + up_ref[...].astype(F32)).astype(BF16)
    own_out[...] = unpacked(key_ref[0], back_ref, each) + coarse_ref[...]


def fine_kernel(each, used, per_row, joins, tile, rows_ref, w_ref, *refs):
    if joins:
        ahead_ref, grad_ref, mem_ref, loss_ref, back_ref = refs
    else:
        grad_ref, mem_ref, loss_ref, head_ref, back_ref = refs
    slots = rows_ref.shape[0]
    dests = slots // each
    clusters, labels, features = w_ref.shape
    w = w_ref[...].reshape(clusters * labels, features)
    lane = lax.broadcasted_iota(jnp.int32, (dests, each, 128), 2)
    at = lax.broadcasted_iota(jnp.int32, (dests, each, 128), 1)
    lead = rows_ref[:, :128].astype(F32).reshape(dests, each, 128)

    def column(row):
        flat = jnp.sum(jnp.where(at == row, lead, 0.0), axis=1, keepdims=True)
        spread = jnp.where(lane == at, jnp.broadcast_to(flat, lead.shape), 0.0)
        return jnp.sum(spread, axis=2, keepdims=True).reshape(slots, 1).astype(jnp.int32)

    members, truths = column(used), column(used + 1)
    some = tile // each
    losses = jnp.zeros((1, labels), F32)
    grads, owners = [], []
    for t in range(slots // tile):
        here = slice(t * tile, (t + 1) * tile)
        member_l = jnp.broadcast_to(members[here], (tile, labels))
        truth_id = jnp.broadcast_to(truths[here], (tile, labels))
        all_logits = lax.dot_general(rows_ref[here, :], w, NT, preferred_element_type=F32)
        logits = jnp.zeros((tile, labels), F32)
        for m in range(clusters):
            logits = jnp.where(member_l == m, all_logits[:, m * labels : (m + 1) * labels], logits)
        label = lax.broadcasted_iota(jnp.int32, (tile, labels), 1)
        truth = jnp.where(label == truth_id, 1.0, 0.0)
        bce = jnp.maximum(logits, 0.0) + jnp.log1p(jnp.exp(-jnp.abs(logits))) - truth * logits
        row_loss = jnp.sum(bce, axis=1, keepdims=True) / (per_row * labels)
        losses = losses + jnp.sum(
            jnp.where(label == member_l, jnp.broadcast_to(row_loss, (tile, labels)), 0.0),
            axis=0,
            keepdims=True,
        )
        grad = ((jax.nn.sigmoid(logits) - truth) / per_row).astype(BF16).astype(F32)
        wide = jnp.concatenate(
            [jnp.where(member_l == m, grad, 0.0).astype(BF16) for m in range(clusters)], axis=1
        )
        back = jnp.dot(wide, w, preferred_element_type=F32).reshape(some, each, features)
        if joins:
            ahead = ahead_ref[t * some * 24 : (t + 1) * some * 24, :].astype(F32)
            back = jnp.concatenate([ahead.reshape(some, 24, features), back], axis=1)
            n = some * (each + 24)
            back_ref[t * n : (t + 1) * n, :] = back.reshape(n, features).astype(BF16)
        else:
            n = some * 24
            head_ref[t * n : (t + 1) * n, :] = back[:, :24].reshape(n, features).astype(BF16)
            n = some * (each - 24)
            back_ref[t * n : (t + 1) * n, :] = back[:, 24:].reshape(n, features).astype(BF16)
        grads.append(grad)
        owners.append(member_l.astype(F32))
    grad_ref[...] = jnp.concatenate(grads, axis=0).T.astype(BF16)
    mem_ref[...] = jnp.concatenate(owners, axis=0).T[:8].astype(jnp.int32)

    @pl.when(pl.program_id(0) == 0)
    def _():
        loss_ref[...] = jnp.zeros(loss_ref.shape, F32)

    loss_ref[...] += jnp.broadcast_to(losses, loss_ref.shape)


def fine_part(rows, weight, ahead, each, used, per_row, step, tile, name):
    slots, features = rows.shape
    clusters, labels, _ = weight.shape
    joins = ahead is not None
    sizes = [each + 24] if joins else [24, each - 24]
    dests = step // each
    block = lambda n: pl.BlockSpec((dests * n, features), lambda i: (i, 0))
    return pl.pallas_call(
        lambda *r: fine_kernel(each, used, per_row, joins, tile, *r),
        grid=(slots // step,),
        out_shape=[
            sds((labels, slots), BF16),
            sds((8, slots), jnp.int32),
            sds((8, 128), F32),
            *(sds((slots // each * n, features), BF16) for n in sizes),
        ],
        in_specs=[block(each), whole(weight)] + ([block(24)] if joins else []),
        out_specs=[
            pl.BlockSpec((labels, step), lambda i: (0, i)),
            pl.BlockSpec((8, step), lambda i: (0, i)),
            pl.BlockSpec((8, 128), lambda i: (0, 0)),
            *(block(n) for n in sizes),
        ],
        compiler_params=pltpu.CompilerParams(vmem_limit_bytes=LIMIT),
        cost_estimate=COST,
        name=name,
    )(*((rows, weight, ahead) if joins else (rows, weight)))


def weight_kernel(*refs):
    grads, mems, rows, out_ref = refs[:2], refs[2:4], refs[4:6], refs[6]
    each, labels, features = out_ref.shape
    first = pl.program_id(0) * each
    total = None
    for g_ref, m_ref, r_ref in zip(grads, mems, rows):
        grad = g_ref[...].astype(F32)
        mem = jnp.broadcast_to(m_ref[:1, :], grad.shape)
        wide = jnp.concatenate(
            [jnp.where(mem == first + m, grad, 0.0).astype(BF16) for m in range(each)], axis=0
        )
        part = jnp.dot(wide, r_ref[...], preferred_element_type=F32)
        total = part if total is None else total + part
    out_ref[...] = total.astype(BF16).reshape(out_ref.shape)


def coarse_kernel(target_ref, rows_ref, w_ref, loss_ref, back_ref):
    w = w_ref[...]
    scores = lax.dot_general(rows_ref[...], w, NT, preferred_element_type=F32)
    column = lax.broadcasted_iota(jnp.int32, scores.shape, 1)
    is_target = column == jnp.broadcast_to(target_ref[:, :1], scores.shape)
    top = jnp.max(scores, axis=1, keepdims=True)
    lifted = jnp.exp(scores - top)
    total = jnp.sum(lifted, axis=1, keepdims=True)
    at_target = jnp.sum(jnp.where(is_target, scores, 0.0), axis=1, keepdims=True)
    grad = (lifted * (1.0 / total) - jnp.where(is_target, 1.0, 0.0)).astype(BF16)
    back_ref[...] = jnp.dot(grad, w, preferred_element_type=F32)
    loss_ref[...] = jnp.broadcast_to(top + jnp.log(total) - at_target, loss_ref.shape)


def coarse_part(target, rows, weight):
    own, features = rows.shape
    tile = 128
    return pl.pallas_call(
        coarse_kernel,
        grid=(own // tile,),
        out_shape=[sds((own, 128), F32), sds((own, features), F32)],
        in_specs=[
            pl.BlockSpec((tile, 128), lambda i: (i, 0)),
            pl.BlockSpec((tile, features), lambda i: (i, 0)),
            pl.BlockSpec(weight.shape, lambda i: (0, 0), pipeline_mode=pl.Buffered(1)),
        ],
        out_specs=[
            pl.BlockSpec((tile, 128), lambda i: (i, 0)),
            pl.BlockSpec((tile, features), lambda i: (i, 0)),
        ],
        compiler_params=pltpu.CompilerParams(vmem_limit_bytes=LIMIT),
        cost_estimate=COST,
        name="coarse",
    )(jnp.broadcast_to(target[:, None], (own, 128)), rows, weight)


def weight_part(grads, mems, rows, shape):
    clusters, labels, features = shape
    each = 4
    const = lambda a: pl.BlockSpec(a.shape, lambda i: (0, 0), pipeline_mode=pl.Buffered(1))
    args = (*grads, *mems, *rows)
    return pl.pallas_call(
        weight_kernel,
        grid=(clusters // each,),
        out_shape=sds(shape, BF16),
        in_specs=[const(a) for a in args],
        out_specs=pl.BlockSpec((each, labels, features), lambda i: (i, 0, 0)),
        compiler_params=pltpu.CompilerParams(vmem_limit_bytes=LIMIT),
        cost_estimate=COST,
        name="weights",
    )(*args)


def per_device(encoded, coarse_weight, fine_weight, cluster_group, cluster_member, positive):
    own, features = encoded.shape
    clusters, labels, _ = fine_weight.shape
    per_row = cluster_group.shape[1]
    n_z = lax.axis_size("z")
    plane = lax.axis_size(PLANE)
    each_row = lax.axis_size("y") * lax.axis_size("c")
    z = lax.axis_index("z")
    half = own // 2

    def shift(value, by):
        return lax.ppermute(value, "z", [(i, (i + by) % n_z) for i in range(n_z)])

    def exchange(value):
        slots = value.shape[0]
        cube = value.reshape(plane, slots // plane, features)
        return lax.all_to_all(cube, PLANE, 0, 0, tiled=True).reshape(slots, features)

    label = jnp.where(jnp.arange(per_row)[None, :] == 0, positive[:, None], 255)
    meta = jnp.concatenate([cluster_group, cluster_member, label], axis=0).astype(BF16).T
    source = jnp.concatenate([encoded, meta], axis=0)
    up1, down1 = shift(source, 1), shift(source, -1)
    up2, down2 = shift(up1, 1), shift(down1, -1)

    gathered = coarse_weight
    for axis in ("c", "y", "x"):
        n = lax.axis_size(axis)
        turns = [
            lax.ppermute(gathered, axis, [(i, (i - d) % n) for i in range(n)]) for d in range(1, n)
        ]
        gathered = jnp.concatenate([gathered, *turns], axis=0)

    dest = jnp.arange(plane, dtype=jnp.int32)
    gid = (dest // each_row) * (each_row * n_z) + z * each_row + dest % each_row
    gid = jnp.broadcast_to(gid[:, None], (plane, 128)).astype(F32)

    keys_of = lambda n: sds((n, plane, own), jnp.int32)

    gathered, gid = lax.optimization_barrier((gathered, gid))
    tail, key_tail = call(
        lambda *r: pack_kernel((1, 1, 1), 24, *r),
        [sds((plane * 40, features), BF16), keys_of(3)],
        (gid, source, up1, down1),
        "pack_tail",
    )
    near, key_head = call(
        join_kernel,
        [sds((plane * 64, features), BF16), keys_of(2)],
        (gid, up2, down2, tail),
        "pack_near",
    )
    up2, down2, near = lax.optimization_barrier((up2, down2, near))
    up3, down3 = shift(up2, 1), shift(down2, -1)
    far_up, far_down = shift(up3[:half], 1), shift(down3[half:], -1)
    far, key_far = call(
        lambda *r: pack_kernel((1, 1, 2), 0, *r),
        [sds((plane * 40, features), BF16), keys_of(3)],
        (gid, up3, down3, far_up, far_down),
        "pack_far",
    )
    rows_near = exchange(near)

    gathered, rows_near = lax.optimization_barrier((gathered, rows_near))
    full_weight = lax.all_gather(gathered, "z", axis=0, tiled=True)
    far, rows_near = lax.optimization_barrier((far, rows_near))
    rows_far = exchange(far)
    grad_near, mem_near, loss_near, head, back_tail = fine_part(
        rows_near, fine_weight, None, 64, 5 * CAP, per_row, 1024, 256, "fine_near"
    )
    rows_far, head, back_tail = lax.optimization_barrier((rows_far, head, back_tail))
    grad_far, mem_far, loss_far, back_far = fine_part(
        rows_far, fine_weight, head, 40, 3 * CAP, per_row, 640, 320, "fine_far"
    )
    cluster_loss = (loss_near + loss_far)[0, :clusters]

    back_far = exchange(back_far)
    d_fine = weight_part(
        [grad_near, grad_far], [mem_near, mem_far], [rows_near, rows_far], fine_weight.shape
    )
    group = cluster_group[:, 0]
    x, y, c = (lax.axis_index(axis) for axis in PLANE)
    n_x, n_y, n_c = (lax.axis_size(axis) for axis in PLANE)
    from_x = (group // (each_row * n_z) - x) % n_x
    from_y = (group // n_c - y) % n_y
    from_c = (group - c) % n_c
    at_z = group // each_row % n_z
    place = (((at_z * n_x + from_x) * n_y + from_y) * n_c + from_c) * clusters + cluster_member[:, 0]
    row_loss, coarse_back = coarse_part(place, encoded, full_weight)
    back_tail, back_far, d_fine, coarse_back = lax.optimization_barrier(
        (back_tail, back_far, d_fine, coarse_back)
    )
    back_tail = exchange(back_tail)
    at_m3, at_3, at_4 = call(
        lambda *r: unpack_far_kernel(24, *r),
        [sds((own, features), F32)] * 2 + [sds((own, features), BF16)],
        (key_far, back_far),
        "unpack_far",
    )
    at_m2, at_2 = call(
        lambda *r: unpack_far_kernel(0, *r),
        [sds((own, features), F32)] * 2,
        (key_head, back_far),
        "unpack_head",
    )
    got_down, got_up = shift(at_4[:half], -1), shift(at_4[half:], 1)
    go_down = at_m3 + jnp.pad(got_down.astype(F32), ((0, half), (0, 0)))
    go_up = at_3 + jnp.pad(got_up.astype(F32), ((half, 0), (0, 0)))
    go_down = at_m2 + shift(go_down.astype(BF16), -1).astype(F32)
    go_up = at_2 + shift(go_up.astype(BF16), 1).astype(F32)
    got_down, got_up = shift(go_down.astype(BF16), -1), shift(go_up.astype(BF16), 1)
    mine, go_down, go_up = call(
        lambda *r: unpack_near_kernel(40, *r),
        [sds((own, features), F32)] + [sds((own, features), BF16)] * 2,
        (key_tail, back_tail, coarse_back, got_down, got_up),
        "unpack_near",
    )
    got_down, got_up = shift(go_down, -1).astype(F32), shift(go_up, 1).astype(F32)
    d_encoded = (mine + got_down + got_up).astype(BF16)
    return row_loss[:, 0], d_encoded, d_fine, cluster_loss


def solution(mesh):
    fine_mesh = Mesh(mesh.devices.reshape(4, 8, 4, 2), EVERY)
    rows = P(EVERY)
    wide = P(EVERY, None)
    cube = P(EVERY, None, None)
    return jax.shard_map(
        per_device,
        mesh=fine_mesh,
        in_specs=(wide, wide, cube, wide, wide, rows),
        out_specs=(rows, wide, cube, rows),
        check_vma=False,
    )
```

```python
import jax
import jax.numpy as jnp
from jax import lax
from jax.experimental import pallas as pl
from jax.experimental.pallas import tpu as pltpu
from jax.sharding import Mesh, PartitionSpec as P

CAP = 12
LIMIT = 56 * 2**20
PACKED = pl.CostEstimate(flops=4000000000, bytes_accessed=6 * 10**6, transcendentals=0)
COST = pl.CostEstimate(flops=1, bytes_accessed=1, transcendentals=0)
EMPTY = 128
PLANE = ("x", "y", "c")
EVERY = ("x", "z", "y", "c")
F32 = jnp.float32
BF16 = jnp.bfloat16
NT = (((1,), (1,)), ((), ()))
TN = (((0,), (0,)), ((), ()))


def whole(a):
    return pl.BlockSpec(a.shape, lambda i: (0,) * len(a.shape), pipeline_mode=pl.Buffered(1))


def call(kernel, out_shape, args, name):
    return pl.pallas_call(
        kernel,
        grid=(1,),
        out_shape=out_shape,
        in_specs=[whole(a) for a in args],
        out_specs=[whole(o) for o in out_shape],
        compiler_params=pltpu.CompilerParams(vmem_limit_bytes=LIMIT),
        cost_estimate=PACKED if name.startswith("pack_far") else COST,
        name=name,
    )(*args)


def sds(shape, dtype):
    return jax.ShapeDtypeStruct(shape, dtype)


def source_kernel(rows_ref, group_ref, member_ref, positive_ref, out_ref):
    rows = rows_ref.shape[0]
    out_ref[:rows, :] = rows_ref[...]
    slot = lax.broadcasted_iota(jnp.int32, group_ref.shape, 0)
    label = jnp.where(slot == 0, jnp.broadcast_to(positive_ref[...], slot.shape), 255)
    for i, part in enumerate((group_ref[...], member_ref[...], label)):
        out_ref[rows:, i * rows : (i + 1) * rows] = part.astype(F32).astype(BF16)


def plan(meta, gid, upper):
    dests, rows = gid.shape
    group, member, label = meta[:, :rows], meta[:, rows : 2 * rows], meta[:, 2 * rows :]
    load = member * 256.0 + label + 1.0
    val = jnp.zeros((dests, rows), F32)
    for s in range(meta.shape[0]):
        val = val + jnp.where(group[s : s + 1, :] == gid, load[s : s + 1, :], 0.0)
    hit = jnp.where(val > 0.0, 1.0, 0.0).astype(BF16)
    rank = jnp.dot(hit, upper, preferred_element_type=F32)
    return val, jnp.where(val > 0.0, rank, -1.0).astype(jnp.int32)


def one_hot(key, each):
    dests, rows = key.shape
    at = lax.broadcasted_iota(jnp.int32, (dests, each, rows), 1)
    hot = jnp.where(jnp.broadcast_to(key[:, None, :], at.shape) == at, 1.0, 0.0)
    return hot.reshape(dests * each, rows).astype(BF16)


def packed(pieces, each, lane0, used, gid_ref, rows_refs, key_ref):
    _, dests, rows = key_ref.shape
    gid = jnp.broadcast_to(gid_ref[:, :1], (dests, rows))
    upper = jnp.where(
        lax.broadcasted_iota(jnp.int32, (rows, rows), 0)
        < lax.broadcasted_iota(jnp.int32, (rows, rows), 1),
        1.0,
        0.0,
    ).astype(BF16)
    lanes = lax.broadcasted_iota(jnp.int32, (dests, 128), 1)
    codes = jnp.zeros((dests, 128), F32)
    total, first = None, 0
    for i, count in enumerate(pieces):
        mine = rows_refs[first : first + count]
        first += count
        size = mine[-1].shape[0]
        val, slot = plan(mine[-1][size - 8 :, :].astype(F32), gid, upper)
        for k in range(CAP):
            found = jnp.sum(jnp.where(slot == k, val, 0.0), axis=1, keepdims=True)
            codes = jnp.where(lanes == lane0 + i * CAP + k, found, codes)
        key = jnp.where(slot >= 0, slot + i * CAP, -1)
        key_ref[i] = key
        hot = one_hot(key, each)
        start = 0
        for r in mine:
            count_rows = min(r.shape[0], rows - start)
            part = jnp.dot(
                hot[:, start : start + count_rows],
                r[:count_rows, :],
                preferred_element_type=F32,
            )
            total = part if total is None else total + part
            start += count_rows
    code = codes.astype(jnp.int32)
    held = (lanes >= lane0) & (lanes < used)
    member = jnp.where(code > 0, (code - 1) >> 8, jnp.where(held, EMPTY, 0)).astype(F32)
    label = jnp.where(code > 0, (code - 1) & 255, 0).astype(F32)
    return total, member, label


def code_rows(member, label, each, row):
    dests = member.shape[0]
    at = lax.broadcasted_iota(jnp.int32, (dests, each, 128), 1)
    return jnp.where(
        at == row,
        jnp.broadcast_to(member[:, None, :], at.shape),
        jnp.where(at == row + 1, jnp.broadcast_to(label[:, None, :], at.shape), 0.0),
    ).reshape(dests * each, 128)


def pack_kernel(pieces, lane0, gid_ref, *refs):
    rows_refs, (out_ref, key_ref) = refs[:-2], refs[-2:]
    total, member, label = packed(pieces, 40, lane0, 128, gid_ref, rows_refs, key_ref)
    extra = code_rows(member, label, 40, 3 * CAP)
    out_ref[:, :128] = (total[:, :128] + extra).astype(BF16)
    out_ref[:, 128:] = total[:, 128:].astype(BF16)


def join_kernel(gid_ref, up_ref, down_ref, tail_ref, out_ref, key_ref):
    dests = gid_ref.shape[0]
    total, member, label = packed((1, 1), 24, 0, 24, gid_ref, (up_ref, down_ref), key_ref)
    extra = code_rows(member, label, 40, 3 * CAP)
    tail = tail_ref[...].astype(F32)
    for lo, hi in ((0, 128), (128, total.shape[1])):
        end = tail[:, lo:hi] + extra if lo == 0 else tail[:, lo:hi]
        both = jnp.concatenate(
            [total[:, lo:hi].reshape(dests, 24, hi - lo), end.reshape(dests, 40, hi - lo)], axis=1
        )
        out_ref[:, lo:hi] = both.reshape(dests * 64, hi - lo).astype(BF16)


def unpacked(key, back_ref, each):
    return lax.dot_general(one_hot(key, each), back_ref[...], TN, preferred_element_type=F32)


def unpack_far_kernel(offset, which, key_ref, back_ref, *outs):
    for i, out in zip(which, outs):
        key = jnp.where(key_ref[i] >= 0, key_ref[i] + offset, -1)
        out[...] = unpacked(key, back_ref, 64).astype(out.dtype)


def unpack_near_kernel(each, key_ref, back_ref, coarse_ref, down_ref, up_ref, own_out, down_out, up_out):
    down_out[...] = (unpacked(key_ref[1], back_ref, each) + down_ref[...].astype(F32)).astype(BF16)
    up_out[...] = (unpacked(key_ref[2], back_ref, each) + up_ref[...].astype(F32)).astype(BF16)
    own_out[...] = unpacked(key_ref[0], back_ref, each) + coarse_ref[...]


def fine_kernel(each, used, per_row, joins, tile, rows_ref, w_ref, *refs):
    if joins:
        ahead_ref, grad_ref, mem_ref, loss_ref, back_ref = refs
    else:
        grad_ref, mem_ref, loss_ref, head_ref, back_ref = refs
    slots = rows_ref.shape[0]
    dests = slots // each
    clusters, labels, features = w_ref.shape
    w = w_ref[...].reshape(clusters * labels, features)
    lane = lax.broadcasted_iota(jnp.int32, (dests, each, 128), 2)
    at = lax.broadcasted_iota(jnp.int32, (dests, each, 128), 1)
    lead = rows_ref[:, :128].astype(F32).reshape(dests, each, 128)

    def column(row):
        flat = jnp.sum(jnp.where(at == row, lead, 0.0), axis=1, keepdims=True)
        spread = jnp.where(lane == at, jnp.broadcast_to(flat, lead.shape), 0.0)
        return jnp.sum(spread, axis=2, keepdims=True).reshape(slots, 1).astype(jnp.int32)

    members, truths = column(used), column(used + 1)
    some = tile // each
    losses = jnp.zeros((1, labels), F32)
    grads, owners = [], []
    for t in range(slots // tile):
        here = slice(t * tile, (t + 1) * tile)
        member_l = jnp.broadcast_to(members[here], (tile, labels))
        truth_id = jnp.broadcast_to(truths[here], (tile, labels))
        all_logits = lax.dot_general(rows_ref[here, :], w, NT, preferred_element_type=F32)
        logits = jnp.zeros((tile, labels), F32)
        for m in range(clusters):
            logits = jnp.where(member_l == m, all_logits[:, m * labels : (m + 1) * labels], logits)
        label = lax.broadcasted_iota(jnp.int32, (tile, labels), 1)
        truth = jnp.where(label == truth_id, 1.0, 0.0)
        bce = jnp.maximum(logits, 0.0) + jnp.log1p(jnp.exp(-jnp.abs(logits))) - truth * logits
        row_loss = jnp.sum(bce, axis=1, keepdims=True) / (per_row * labels)
        losses = losses + jnp.sum(
            jnp.where(label == member_l, jnp.broadcast_to(row_loss, (tile, labels)), 0.0),
            axis=0,
            keepdims=True,
        )
        grad = ((jax.nn.sigmoid(logits) - truth) / per_row).astype(BF16).astype(F32)
        wide = jnp.concatenate(
            [jnp.where(member_l == m, grad, 0.0).astype(BF16) for m in range(clusters)], axis=1
        )
        back = jnp.dot(wide, w, preferred_element_type=F32).reshape(some, each, features)
        if joins:
            ahead = ahead_ref[t * some * 24 : (t + 1) * some * 24, :].astype(F32)
            back = jnp.concatenate([ahead.reshape(some, 24, features), back], axis=1)
            n = some * (each + 24)
            back_ref[t * n : (t + 1) * n, :] = back.reshape(n, features).astype(BF16)
        else:
            n = some * 24
            head_ref[t * n : (t + 1) * n, :] = back[:, :24].reshape(n, features).astype(BF16)
            n = some * (each - 24)
            back_ref[t * n : (t + 1) * n, :] = back[:, 24:].reshape(n, features).astype(BF16)
        grads.append(grad)
        owners.append(member_l.astype(F32))
    grad_ref[...] = jnp.concatenate(grads, axis=0).T.astype(BF16)
    mem_ref[...] = jnp.concatenate(owners, axis=0).T[:8].astype(jnp.int32)

    @pl.when(pl.program_id(0) == 0)
    def _():
        loss_ref[...] = jnp.zeros(loss_ref.shape, F32)

    loss_ref[...] += jnp.broadcast_to(losses, loss_ref.shape)


def fine_part(rows, weight, ahead, each, used, per_row, step, tile, name):
    slots, features = rows.shape
    clusters, labels, _ = weight.shape
    joins = ahead is not None
    sizes = [each + 24] if joins else [24, each - 24]
    dests = step // each
    block = lambda n: pl.BlockSpec((dests * n, features), lambda i: (i, 0))
    return pl.pallas_call(
        lambda *r: fine_kernel(each, used, per_row, joins, tile, *r),
        grid=(slots // step,),
        out_shape=[
            sds((labels, slots), BF16),
            sds((8, slots), jnp.int32),
            sds((8, 128), F32),
            *(sds((slots // each * n, features), BF16) for n in sizes),
        ],
        in_specs=[block(each), whole(weight)] + ([block(24)] if joins else []),
        out_specs=[
            pl.BlockSpec((labels, step), lambda i: (0, i)),
            pl.BlockSpec((8, step), lambda i: (0, i)),
            pl.BlockSpec((8, 128), lambda i: (0, 0)),
            *(block(n) for n in sizes),
        ],
        compiler_params=pltpu.CompilerParams(vmem_limit_bytes=LIMIT),
        cost_estimate=COST,
        name=name,
    )(*((rows, weight, ahead) if joins else (rows, weight)))


def weight_kernel(*refs):
    grads, mems, rows, out_ref = refs[:2], refs[2:4], refs[4:6], refs[6]
    each, labels, features = out_ref.shape
    first = pl.program_id(0) * each
    total = None
    for g_ref, m_ref, r_ref in zip(grads, mems, rows):
        grad = g_ref[...].astype(F32)
        mem = jnp.broadcast_to(m_ref[:1, :], grad.shape)
        wide = jnp.concatenate(
            [jnp.where(mem == first + m, grad, 0.0).astype(BF16) for m in range(each)], axis=0
        )
        part = jnp.dot(wide, r_ref[...], preferred_element_type=F32)
        total = part if total is None else total + part
    out_ref[...] = total.astype(BF16).reshape(out_ref.shape)


def coarse_kernel(target_ref, rows_ref, *refs):
    w_refs, (loss_ref, back_ref) = refs[:-2], refs[-2:]
    rows = rows_ref[...]
    scores = jnp.concatenate(
        [lax.dot_general(rows, w[...], NT, preferred_element_type=F32) for w in w_refs], axis=1
    )
    column = lax.broadcasted_iota(jnp.int32, scores.shape, 1)
    is_target = column == jnp.broadcast_to(target_ref[...], scores.shape)
    top = jnp.max(scores, axis=1, keepdims=True)
    lifted = jnp.exp(scores - top)
    total = jnp.sum(lifted, axis=1, keepdims=True)
    at_target = jnp.sum(jnp.where(is_target, scores, 0.0), axis=1, keepdims=True)
    grad = (lifted * (1.0 / total) - jnp.where(is_target, 1.0, 0.0)).astype(BF16)
    back, start = None, 0
    for w in w_refs:
        part = jnp.dot(grad[:, start : start + w.shape[0]], w[...], preferred_element_type=F32)
        back = part if back is None else back + part
        start += w.shape[0]
    back_ref[...] = back
    loss_ref[...] = top + jnp.log(total) - at_target


def coarse_part(target, rows, weights):
    own, features = rows.shape
    tile = 128
    column = pl.BlockSpec((tile, 1), lambda i: (i, 0))
    block = pl.BlockSpec((tile, features), lambda i: (i, 0))
    return pl.pallas_call(
        coarse_kernel,
        grid=(own // tile,),
        out_shape=[sds((own, 1), F32), sds((own, features), F32)],
        in_specs=[column, block, *(whole(w) for w in weights)],
        out_specs=[column, block],
        compiler_params=pltpu.CompilerParams(vmem_limit_bytes=LIMIT),
        cost_estimate=COST,
        name="coarse",
    )(target[:, None], rows, *weights)


def weight_part(grads, mems, rows, shape):
    clusters, labels, features = shape
    each = 4
    const = lambda a: pl.BlockSpec(a.shape, lambda i: (0, 0), pipeline_mode=pl.Buffered(1))
    args = (*grads, *mems, *rows)
    return pl.pallas_call(
        weight_kernel,
        grid=(clusters // each,),
        out_shape=sds(shape, BF16),
        in_specs=[const(a) for a in args],
        out_specs=pl.BlockSpec((each, labels, features), lambda i: (i, 0, 0)),
        compiler_params=pltpu.CompilerParams(vmem_limit_bytes=LIMIT),
        cost_estimate=COST,
        name="weights",
    )(*args)


def per_device(encoded, coarse_weight, fine_weight, cluster_group, cluster_member, positive):
    own, features = encoded.shape
    clusters, labels, _ = fine_weight.shape
    per_row = cluster_group.shape[1]
    n_z = lax.axis_size("z")
    plane = lax.axis_size(PLANE)
    each_row = lax.axis_size("y") * lax.axis_size("c")
    z = lax.axis_index("z")
    half = own // 2

    def shift(value, by):
        return lax.ppermute(value, "z", [(i, (i + by) % n_z) for i in range(n_z)])

    def exchange(value):
        slots = value.shape[0]
        cube = value.reshape(plane, slots // plane, features)
        return lax.all_to_all(cube, PLANE, 0, 0, tiled=True).reshape(slots, features)

    (source,) = call(
        source_kernel,
        [sds((own + per_row, features), BF16)],
        (encoded, cluster_group.T, cluster_member.T, positive[None, :]),
        "source",
    )
    up1, down1 = shift(source, 1), shift(source, -1)
    up2, down2 = shift(up1, 1), shift(down1, -1)

    def turned(value, axis):
        n = lax.axis_size(axis)
        turns = [
            lax.ppermute(value, axis, [(i, (i - d) % n) for i in range(n)]) for d in range(1, n)
        ]
        return jnp.concatenate([value, *turns], axis=0)

    gathered = turned(turned(coarse_weight, "c"), "y")

    dest = jnp.arange(plane, dtype=jnp.int32)
    gid = (dest // each_row) * (each_row * n_z) + z * each_row + dest % each_row
    gid = jnp.broadcast_to(gid[:, None], (plane, 128)).astype(F32)

    keys_of = lambda n: sds((n, plane, own), jnp.int32)

    tail, key_tail = call(
        lambda *r: pack_kernel((1, 1, 1), 24, *r),
        [sds((plane * 40, features), BF16), keys_of(3)],
        (gid, source, up1, down1),
        "pack_tail",
    )
    gathered, tail = lax.optimization_barrier((turned(gathered, "x"), tail))
    near, key_head = call(
        join_kernel,
        [sds((plane * 64, features), BF16), keys_of(2)],
        (gid, up2, down2, tail),
        "pack_near",
    )
    up2, down2, near = lax.optimization_barrier((up2, down2, near))
    up3, down3 = shift(up2, 1), shift(down2, -1)
    far_up, far_down = shift(up3[:half], 1), shift(down3[half:], -1)
    far, key_far = call(
        lambda *r: pack_kernel((1, 1, 2), 0, *r),
        [sds((plane * 40, features), BF16), keys_of(3)],
        (gid, up3, down3, far_up, far_down),
        "pack_far",
    )
    rows_near = exchange(near)

    gathered, rows_near = lax.optimization_barrier((gathered, rows_near))
    weights = [gathered, shift(gathered, 1), shift(gathered, -1)]
    far, rows_near = lax.optimization_barrier((far, rows_near))
    rows_far = exchange(far)
    grad_near, mem_near, loss_near, head, back_tail = fine_part(
        rows_near, fine_weight, None, 64, 5 * CAP, per_row, 1024, 256, "fine_near"
    )
    *weights[1:3], head = lax.optimization_barrier((*weights[1:3], head))
    weights += [shift(weights[1], 1), shift(weights[2], -1)]
    grad_far, mem_far, loss_far, back_far = fine_part(
        rows_far, fine_weight, head, 40, 3 * CAP, per_row, 640, 320, "fine_far"
    )
    *weights[3:5], back_far = lax.optimization_barrier((*weights[3:5], back_far))
    weights += [shift(weights[3], 1), shift(weights[4], -1)]
    part = gathered.shape[0] // 2
    weights += [shift(weights[5][:part], 1), shift(weights[6][part:], -1)]
    cluster_loss = (loss_near + loss_far)[0, :clusters]

    back_far = exchange(back_far)
    d_fine = weight_part(
        [grad_near, grad_far], [mem_near, mem_far], [rows_near, rows_far], fine_weight.shape
    )
    group = cluster_group[:, 0]
    x, y, c = (lax.axis_index(axis) for axis in PLANE)
    n_x, n_y, n_c = (lax.axis_size(axis) for axis in PLANE)
    from_x = (group // (each_row * n_z) - x) % n_x
    from_y = (group // n_c - y) % n_y
    from_c = (group - c) % n_c
    from_z = (group // each_row - z) % n_z
    at_z = jnp.where(from_z < n_z // 2, 2 * from_z, 2 * (n_z - from_z) - 1)
    place = (((at_z * n_x + from_x) * n_y + from_y) * n_c + from_c) * clusters + cluster_member[:, 0]
    row_loss, coarse_back = coarse_part(place, encoded, weights)
    back_tail, back_far, d_fine, coarse_back = lax.optimization_barrier(
        (back_tail, back_far, d_fine, coarse_back)
    )
    back_tail = exchange(back_tail)
    (at_4,) = call(
        lambda *r: unpack_far_kernel(24, (2,), *r),
        [sds((own, features), BF16)],
        (key_far, back_far),
        "unpack_4",
    )
    at_m3, at_3 = call(
        lambda *r: unpack_far_kernel(24, (0, 1), *r),
        [sds((own, features), F32)] * 2,
        (key_far, back_far),
        "unpack_far",
    )
    at_m2, at_2 = call(
        lambda *r: unpack_far_kernel(0, (0, 1), *r),
        [sds((own, features), F32)] * 2,
        (key_head, back_far),
        "unpack_head",
    )
    got_down, got_up = shift(at_4[:half], -1), shift(at_4[half:], 1)
    go_down = at_m3 + jnp.pad(got_down.astype(F32), ((0, half), (0, 0)))
    go_up = at_3 + jnp.pad(got_up.astype(F32), ((half, 0), (0, 0)))
    go_down = at_m2 + shift(go_down.astype(BF16), -1).astype(F32)
    go_up = at_2 + shift(go_up.astype(BF16), 1).astype(F32)
    got_down, got_up = shift(go_down.astype(BF16), -1), shift(go_up.astype(BF16), 1)
    mine, go_down, go_up = call(
        lambda *r: unpack_near_kernel(40, *r),
        [sds((own, features), F32)] + [sds((own, features), BF16)] * 2,
        (key_tail, back_tail, coarse_back, got_down, got_up),
        "unpack_near",
    )
    got_down, got_up = shift(go_down, -1).astype(F32), shift(go_up, 1).astype(F32)
    d_encoded = (mine + got_down + got_up).astype(BF16)
    return row_loss[:, 0], d_encoded, d_fine, cluster_loss


def solution(mesh):
    fine_mesh = Mesh(mesh.devices.reshape(4, 8, 4, 2), EVERY)
    rows = P(EVERY)
    wide = P(EVERY, None)
    cube = P(EVERY, None, None)
    return jax.shard_map(
        per_device,
        mesh=fine_mesh,
        in_specs=(wide, wide, cube, wide, wide, rows),
        out_specs=(rows, wide, cube, rows),
        check_vma=False,
    )
```

```python
import jax
import jax.numpy as jnp
from jax import lax
from jax.experimental import pallas as pl
from jax.experimental.pallas import tpu as pltpu
from jax.sharding import Mesh, PartitionSpec as P

CAP = 12
LIMIT = 56 * 2**20
PACKED = pl.CostEstimate(flops=4000000000, bytes_accessed=6 * 10**6, transcendentals=0)
COST = pl.CostEstimate(flops=1, bytes_accessed=1, transcendentals=0)
EMPTY = 128
PLANE = ("x", "y", "c")
EVERY = ("x", "z", "y", "c")
F32 = jnp.float32
BF16 = jnp.bfloat16
NT = (((1,), (1,)), ((), ()))
TN = (((0,), (0,)), ((), ()))


def whole(a):
    return pl.BlockSpec(a.shape, lambda i: (0,) * len(a.shape), pipeline_mode=pl.Buffered(1))


def call(kernel, out_shape, args, name):
    return pl.pallas_call(
        kernel,
        grid=(1,),
        out_shape=out_shape,
        in_specs=[whole(a) for a in args],
        out_specs=[whole(o) for o in out_shape],
        compiler_params=pltpu.CompilerParams(vmem_limit_bytes=LIMIT),
        cost_estimate=PACKED if name.startswith("pack_far") else COST,
        name=name,
    )(*args)


def sds(shape, dtype):
    return jax.ShapeDtypeStruct(shape, dtype)


def source_kernel(rows_ref, group_ref, member_ref, positive_ref, out_ref):
    rows = rows_ref.shape[0]
    out_ref[:rows, :] = rows_ref[...]
    slot = lax.broadcasted_iota(jnp.int32, group_ref.shape, 0)
    label = jnp.where(slot == 0, jnp.broadcast_to(positive_ref[...], slot.shape), 255)
    for i, part in enumerate((group_ref[...], member_ref[...], label)):
        out_ref[rows:, i * rows : (i + 1) * rows] = part.astype(F32).astype(BF16)


def plan(meta, gid, upper):
    dests, rows = gid.shape
    group, member, label = meta[:, :rows], meta[:, rows : 2 * rows], meta[:, 2 * rows :]
    load = member * 256.0 + label + 1.0
    val = jnp.zeros((dests, rows), F32)
    for s in range(meta.shape[0]):
        val = val + jnp.where(group[s : s + 1, :] == gid, load[s : s + 1, :], 0.0)
    hit = jnp.where(val > 0.0, 1.0, 0.0).astype(BF16)
    rank = jnp.dot(hit, upper, preferred_element_type=F32)
    return val, jnp.where(val > 0.0, rank, -1.0).astype(jnp.int32)


def one_hot(key, each):
    dests, rows = key.shape
    at = lax.broadcasted_iota(jnp.int32, (dests, each, rows), 1)
    hot = jnp.where(jnp.broadcast_to(key[:, None, :], at.shape) == at, 1.0, 0.0)
    return hot.reshape(dests * each, rows).astype(BF16)


def packed(pieces, each, lane0, used, gid_ref, rows_refs, key_ref):
    _, dests, rows = key_ref.shape
    gid = jnp.broadcast_to(gid_ref[:, :1], (dests, rows))
    upper = jnp.where(
        lax.broadcasted_iota(jnp.int32, (rows, rows), 0)
        < lax.broadcasted_iota(jnp.int32, (rows, rows), 1),
        1.0,
        0.0,
    ).astype(BF16)
    lanes = lax.broadcasted_iota(jnp.int32, (dests, 128), 1)
    codes = jnp.zeros((dests, 128), F32)
    total, first = None, 0
    for i, count in enumerate(pieces):
        mine = rows_refs[first : first + count]
        first += count
        size = mine[-1].shape[0]
        val, slot = plan(mine[-1][size - 8 :, :].astype(F32), gid, upper)
        for k in range(CAP):
            found = jnp.sum(jnp.where(slot == k, val, 0.0), axis=1, keepdims=True)
            codes = jnp.where(lanes == lane0 + i * CAP + k, found, codes)
        key = jnp.where(slot >= 0, slot + i * CAP, -1)
        key_ref[i] = key
        hot = one_hot(key, each)
        start = 0
        for r in mine:
            count_rows = min(r.shape[0], rows - start)
            part = jnp.dot(
                hot[:, start : start + count_rows],
                r[:count_rows, :],
                preferred_element_type=F32,
            )
            total = part if total is None else total + part
            start += count_rows
    code = codes.astype(jnp.int32)
    held = (lanes >= lane0) & (lanes < used)
    member = jnp.where(code > 0, (code - 1) >> 8, jnp.where(held, EMPTY, 0)).astype(F32)
    label = jnp.where(code > 0, (code - 1) & 255, 0).astype(F32)
    return total, member, label


def code_rows(member, label, each, row):
    dests = member.shape[0]
    at = lax.broadcasted_iota(jnp.int32, (dests, each, 128), 1)
    return jnp.where(
        at == row,
        jnp.broadcast_to(member[:, None, :], at.shape),
        jnp.where(at == row + 1, jnp.broadcast_to(label[:, None, :], at.shape), 0.0),
    ).reshape(dests * each, 128)


def pack_kernel(pieces, lane0, gid_ref, *refs):
    rows_refs, (out_ref, key_ref) = refs[:-2], refs[-2:]
    total, member, label = packed(pieces, 40, lane0, 128, gid_ref, rows_refs, key_ref)
    extra = code_rows(member, label, 40, 3 * CAP)
    out_ref[:, :128] = (total[:, :128] + extra).astype(BF16)
    out_ref[:, 128:] = total[:, 128:].astype(BF16)


def join_kernel(gid_ref, up_ref, down_ref, tail_ref, out_ref, key_ref):
    dests = gid_ref.shape[0]
    total, member, label = packed((1, 1), 24, 0, 24, gid_ref, (up_ref, down_ref), key_ref)
    extra = code_rows(member, label, 40, 3 * CAP)
    tail = tail_ref[...].astype(F32)
    for lo, hi in ((0, 128), (128, total.shape[1])):
        end = tail[:, lo:hi] + extra if lo == 0 else tail[:, lo:hi]
        both = jnp.concatenate(
            [total[:, lo:hi].reshape(dests, 24, hi - lo), end.reshape(dests, 40, hi - lo)], axis=1
        )
        out_ref[:, lo:hi] = both.reshape(dests * 64, hi - lo).astype(BF16)


def unpacked(key, back_ref, each):
    return lax.dot_general(one_hot(key, each), back_ref[...], TN, preferred_element_type=F32)


def unpack_far_kernel(offset, which, key_ref, back_ref, *outs):
    for i, out in zip(which, outs):
        key = jnp.where(key_ref[i] >= 0, key_ref[i] + offset, -1)
        out[...] = unpacked(key, back_ref, 64).astype(out.dtype)


def unpack_near_kernel(each, key_ref, back_ref, down_ref, up_ref, down_out, up_out):
    down_out[...] = (unpacked(key_ref[1], back_ref, each) + down_ref[...].astype(F32)).astype(BF16)
    up_out[...] = (unpacked(key_ref[2], back_ref, each) + up_ref[...].astype(F32)).astype(BF16)


def unpack_own_kernel(each, key_ref, back_ref, coarse_ref, own_out):
    own_out[...] = unpacked(key_ref[0], back_ref, each) + coarse_ref[...]


def fine_kernel(each, used, per_row, joins, tile, rows_ref, w_ref, *refs):
    if joins:
        ahead_ref, grad_ref, mem_ref, loss_ref, back_ref = refs
    else:
        grad_ref, mem_ref, loss_ref, head_ref, back_ref = refs
    slots = rows_ref.shape[0]
    dests = slots // each
    clusters, labels, features = w_ref.shape
    w = w_ref[...].reshape(clusters * labels, features)
    lane = lax.broadcasted_iota(jnp.int32, (dests, each, 128), 2)
    at = lax.broadcasted_iota(jnp.int32, (dests, each, 128), 1)
    lead = rows_ref[:, :128].astype(F32).reshape(dests, each, 128)

    def column(row):
        flat = jnp.sum(jnp.where(at == row, lead, 0.0), axis=1, keepdims=True)
        spread = jnp.where(lane == at, jnp.broadcast_to(flat, lead.shape), 0.0)
        return jnp.sum(spread, axis=2, keepdims=True).reshape(slots, 1).astype(jnp.int32)

    members, truths = column(used), column(used + 1)
    some = tile // each
    losses = jnp.zeros((1, labels), F32)
    grads, owners = [], []
    for t in range(slots // tile):
        here = slice(t * tile, (t + 1) * tile)
        member_l = jnp.broadcast_to(members[here], (tile, labels))
        truth_id = jnp.broadcast_to(truths[here], (tile, labels))
        all_logits = lax.dot_general(rows_ref[here, :], w, NT, preferred_element_type=F32)
        logits = jnp.zeros((tile, labels), F32)
        for m in range(clusters):
            logits = jnp.where(member_l == m, all_logits[:, m * labels : (m + 1) * labels], logits)
        label = lax.broadcasted_iota(jnp.int32, (tile, labels), 1)
        truth = jnp.where(label == truth_id, 1.0, 0.0)
        bce = jnp.maximum(logits, 0.0) + jnp.log1p(jnp.exp(-jnp.abs(logits))) - truth * logits
        row_loss = jnp.sum(bce, axis=1, keepdims=True) / (per_row * labels)
        losses = losses + jnp.sum(
            jnp.where(label == member_l, jnp.broadcast_to(row_loss, (tile, labels)), 0.0),
            axis=0,
            keepdims=True,
        )
        grad = ((jax.nn.sigmoid(logits) - truth) / per_row).astype(BF16).astype(F32)
        wide = jnp.concatenate(
            [jnp.where(member_l == m, grad, 0.0).astype(BF16) for m in range(clusters)], axis=1
        )
        back = jnp.dot(wide, w, preferred_element_type=F32).reshape(some, each, features)
        if joins:
            ahead = ahead_ref[t * some * 24 : (t + 1) * some * 24, :].astype(F32)
            back = jnp.concatenate([ahead.reshape(some, 24, features), back], axis=1)
            n = some * (each + 24)
            back_ref[t * n : (t + 1) * n, :] = back.reshape(n, features).astype(BF16)
        else:
            n = some * 24
            head_ref[t * n : (t + 1) * n, :] = back[:, :24].reshape(n, features).astype(BF16)
            n = some * (each - 24)
            back_ref[t * n : (t + 1) * n, :] = back[:, 24:].reshape(n, features).astype(BF16)
        grads.append(grad)
        owners.append(member_l.astype(F32))
    grad_ref[...] = jnp.concatenate(grads, axis=0).T.astype(BF16)
    mem_ref[...] = jnp.concatenate(owners, axis=0).T[:8].astype(jnp.int32)

    @pl.when(pl.program_id(0) == 0)
    def _():
        loss_ref[...] = jnp.zeros(loss_ref.shape, F32)

    loss_ref[...] += jnp.broadcast_to(losses, loss_ref.shape)


def fine_part(rows, weight, ahead, each, used, per_row, step, tile, name):
    slots, features = rows.shape
    clusters, labels, _ = weight.shape
    joins = ahead is not None
    sizes = [each + 24] if joins else [24, each - 24]
    dests = step // each
    block = lambda n: pl.BlockSpec((dests * n, features), lambda i: (i, 0))
    return pl.pallas_call(
        lambda *r: fine_kernel(each, used, per_row, joins, tile, *r),
        grid=(slots // step,),
        out_shape=[
            sds((labels, slots), BF16),
            sds((8, slots), jnp.int32),
            sds((8, 128), F32),
            *(sds((slots // each * n, features), BF16) for n in sizes),
        ],
        in_specs=[block(each), whole(weight)] + ([block(24)] if joins else []),
        out_specs=[
            pl.BlockSpec((labels, step), lambda i: (0, i)),
            pl.BlockSpec((8, step), lambda i: (0, i)),
            pl.BlockSpec((8, 128), lambda i: (0, 0)),
            *(block(n) for n in sizes),
        ],
        compiler_params=pltpu.CompilerParams(vmem_limit_bytes=LIMIT),
        cost_estimate=COST,
        name=name,
    )(*((rows, weight, ahead) if joins else (rows, weight)))


def weight_kernel(*refs):
    grads, mems, rows, out_ref = refs[:2], refs[2:4], refs[4:6], refs[6]
    each, labels, features = out_ref.shape
    first = pl.program_id(0) * each
    total = None
    for g_ref, m_ref, r_ref in zip(grads, mems, rows):
        grad = g_ref[...].astype(F32)
        mem = jnp.broadcast_to(m_ref[:1, :], grad.shape)
        wide = jnp.concatenate(
            [jnp.where(mem == first + m, grad, 0.0).astype(BF16) for m in range(each)], axis=0
        )
        part = jnp.dot(wide, r_ref[...], preferred_element_type=F32)
        total = part if total is None else total + part
    out_ref[...] = total.astype(BF16).reshape(out_ref.shape)


def coarse_kernel(target_ref, rows_ref, *refs):
    w_refs, (loss_ref, back_ref) = refs[:-2], refs[-2:]
    rows = rows_ref[...]
    scores = jnp.concatenate(
        [lax.dot_general(rows, w[...], NT, preferred_element_type=F32) for w in w_refs], axis=1
    )
    column = lax.broadcasted_iota(jnp.int32, scores.shape, 1)
    is_target = column == jnp.broadcast_to(target_ref[...], scores.shape)
    top = jnp.max(scores, axis=1, keepdims=True)
    lifted = jnp.exp(scores - top)
    total = jnp.sum(lifted, axis=1, keepdims=True)
    at_target = jnp.sum(jnp.where(is_target, scores, 0.0), axis=1, keepdims=True)
    grad = (lifted * (1.0 / total) - jnp.where(is_target, 1.0, 0.0)).astype(BF16)
    back, start = None, 0
    for w in w_refs:
        part = jnp.dot(grad[:, start : start + w.shape[0]], w[...], preferred_element_type=F32)
        back = part if back is None else back + part
        start += w.shape[0]
    back_ref[...] = back
    loss_ref[...] = top + jnp.log(total) - at_target


def coarse_part(target, rows, weights):
    own, features = rows.shape
    tile = 128
    column = pl.BlockSpec((tile, 1), lambda i: (i, 0))
    block = pl.BlockSpec((tile, features), lambda i: (i, 0))
    return pl.pallas_call(
        coarse_kernel,
        grid=(own // tile,),
        out_shape=[sds((own, 1), F32), sds((own, features), F32)],
        in_specs=[column, block, *(whole(w) for w in weights)],
        out_specs=[column, block],
        compiler_params=pltpu.CompilerParams(vmem_limit_bytes=LIMIT),
        cost_estimate=COST,
        name="coarse",
    )(target[:, None], rows, *weights)


def weight_part(grads, mems, rows, shape):
    clusters, labels, features = shape
    each = 4
    const = lambda a: pl.BlockSpec(a.shape, lambda i: (0, 0), pipeline_mode=pl.Buffered(1))
    args = (*grads, *mems, *rows)
    return pl.pallas_call(
        weight_kernel,
        grid=(clusters // each,),
        out_shape=sds(shape, BF16),
        in_specs=[const(a) for a in args],
        out_specs=pl.BlockSpec((each, labels, features), lambda i: (i, 0, 0)),
        compiler_params=pltpu.CompilerParams(vmem_limit_bytes=LIMIT),
        cost_estimate=COST,
        name="weights",
    )(*args)


def per_device(encoded, coarse_weight, fine_weight, cluster_group, cluster_member, positive):
    own, features = encoded.shape
    clusters, labels, _ = fine_weight.shape
    per_row = cluster_group.shape[1]
    n_z = lax.axis_size("z")
    plane = lax.axis_size(PLANE)
    each_row = lax.axis_size("y") * lax.axis_size("c")
    z = lax.axis_index("z")
    half = own // 2

    def shift(value, by):
        return lax.ppermute(value, "z", [(i, (i + by) % n_z) for i in range(n_z)])

    def exchange(value):
        slots = value.shape[0]
        cube = value.reshape(plane, slots // plane, features)
        return lax.all_to_all(cube, PLANE, 0, 0, tiled=True).reshape(slots, features)

    (source,) = call(
        source_kernel,
        [sds((own + per_row, features), BF16)],
        (encoded, cluster_group.T, cluster_member.T, positive[None, :]),
        "source",
    )
    up1, down1 = shift(source, 1), shift(source, -1)
    up2, down2 = shift(up1, 1), shift(down1, -1)

    def turned(value, axis):
        n = lax.axis_size(axis)
        turns = [
            lax.ppermute(value, axis, [(i, (i - d) % n) for i in range(n)]) for d in range(1, n)
        ]
        return jnp.concatenate([value, *turns], axis=0)

    gathered = turned(turned(coarse_weight, "c"), "y")

    dest = jnp.arange(plane, dtype=jnp.int32)
    gid = (dest // each_row) * (each_row * n_z) + z * each_row + dest % each_row
    gid = jnp.broadcast_to(gid[:, None], (plane, 128)).astype(F32)

    keys_of = lambda n: sds((n, plane, own), jnp.int32)

    tail, key_tail = call(
        lambda *r: pack_kernel((1, 1, 1), 24, *r),
        [sds((plane * 40, features), BF16), keys_of(3)],
        (gid, source, up1, down1),
        "pack_tail",
    )
    gathered, tail = lax.optimization_barrier((turned(gathered, "x"), tail))
    near, key_head = call(
        join_kernel,
        [sds((plane * 64, features), BF16), keys_of(2)],
        (gid, up2, down2, tail),
        "pack_near",
    )
    up2, down2, near = lax.optimization_barrier((up2, down2, near))
    up3, down3 = shift(up2, 1), shift(down2, -1)
    far_up, far_down = shift(up3[:half], 1), shift(down3[half:], -1)
    far, key_far = call(
        lambda *r: pack_kernel((1, 1, 2), 0, *r),
        [sds((plane * 40, features), BF16), keys_of(3)],
        (gid, up3, down3, far_up, far_down),
        "pack_far",
    )
    rows_near = exchange(near)

    gathered, far = lax.optimization_barrier((gathered, far))
    weights = [gathered, shift(gathered, 1), shift(gathered, -1)]
    far, rows_near = lax.optimization_barrier((far, rows_near))
    rows_far = exchange(far)
    *weights[1:3], rows_near = lax.optimization_barrier((*weights[1:3], rows_near))
    weights += [shift(weights[1], 1), shift(weights[2], -1)]
    grad_near, mem_near, loss_near, head, back_tail = fine_part(
        rows_near, fine_weight, None, 64, 5 * CAP, per_row, 1024, 256, "fine_near"
    )
    *weights[3:5], head = lax.optimization_barrier((*weights[3:5], head))
    weights += [shift(weights[3], 1), shift(weights[4], -1)]
    grad_far, mem_far, loss_far, back_far = fine_part(
        rows_far, fine_weight, head, 40, 3 * CAP, per_row, 640, 320, "fine_far"
    )
    *weights[5:7], back_far = lax.optimization_barrier((*weights[5:7], back_far))
    part = gathered.shape[0] // 2
    weights += [shift(weights[5][:part], 1), shift(weights[6][part:], -1)]
    cluster_loss = (loss_near + loss_far)[0, :clusters]

    back_far = exchange(back_far)
    d_fine = weight_part(
        [grad_near, grad_far], [mem_near, mem_far], [rows_near, rows_far], fine_weight.shape
    )
    group = cluster_group[:, 0]
    x, y, c = (lax.axis_index(axis) for axis in PLANE)
    n_x, n_y, n_c = (lax.axis_size(axis) for axis in PLANE)
    from_x = (group // (each_row * n_z) - x) % n_x
    from_y = (group // n_c - y) % n_y
    from_c = (group - c) % n_c
    from_z = (group // each_row - z) % n_z
    at_z = jnp.where(from_z < n_z // 2, 2 * from_z, 2 * (n_z - from_z) - 1)
    place = (((at_z * n_x + from_x) * n_y + from_y) * n_c + from_c) * clusters + cluster_member[:, 0]
    row_loss, coarse_back = coarse_part(place, encoded, weights)
    back_tail, back_far, d_fine, coarse_back = lax.optimization_barrier(
        (back_tail, back_far, d_fine, coarse_back)
    )
    back_tail = exchange(back_tail)
    at_m3, at_3, at_4 = call(
        lambda *r: unpack_far_kernel(24, (0, 1, 2), *r),
        [sds((own, features), F32)] * 2 + [sds((own, features), BF16)],
        (key_far, back_far),
        "unpack_far",
    )
    at_m2, at_2 = call(
        lambda *r: unpack_far_kernel(0, (0, 1), *r),
        [sds((own, features), F32)] * 2,
        (key_head, back_far),
        "unpack_head",
    )
    got_down, got_up = shift(at_4[:half], -1), shift(at_4[half:], 1)
    go_down = at_m3 + jnp.pad(got_down.astype(F32), ((0, half), (0, 0)))
    go_up = at_3 + jnp.pad(got_up.astype(F32), ((half, 0), (0, 0)))
    go_down = at_m2 + shift(go_down.astype(BF16), -1).astype(F32)
    go_up = at_2 + shift(go_up.astype(BF16), 1).astype(F32)
    got_down, got_up = shift(go_down.astype(BF16), -1), shift(go_up.astype(BF16), 1)
    go_down, go_up = call(
        lambda *r: unpack_near_kernel(40, *r),
        [sds((own, features), BF16)] * 2,
        (key_tail, back_tail, got_down, got_up),
        "unpack_near",
    )
    (mine,) = call(
        lambda *r: unpack_own_kernel(40, *r),
        [sds((own, features), F32)],
        (key_tail, back_tail, coarse_back),
        "unpack_own",
    )
    got_down, got_up = shift(go_down, -1).astype(F32), shift(go_up, 1).astype(F32)
    d_encoded = (mine + got_down + got_up).astype(BF16)
    return row_loss[:, 0], d_encoded, d_fine, cluster_loss


def solution(mesh):
    fine_mesh = Mesh(mesh.devices.reshape(4, 8, 4, 2), EVERY)
    rows = P(EVERY)
    wide = P(EVERY, None)
    cube = P(EVERY, None, None)
    return jax.shard_map(
        per_device,
        mesh=fine_mesh,
        in_specs=(wide, wide, cube, wide, wide, rows),
        out_specs=(rows, wide, cube, rows),
        check_vma=False,
    )
```

```python
import jax
import jax.numpy as jnp
from jax import lax
from jax.experimental import pallas as pl
from jax.experimental.pallas import tpu as pltpu
from jax.sharding import Mesh, PartitionSpec as P

CAP = 12
LIMIT = 56 * 2**20
PACKED = pl.CostEstimate(flops=4000000000, bytes_accessed=6 * 10**6, transcendentals=0)
COST = pl.CostEstimate(flops=1, bytes_accessed=1, transcendentals=0)
EMPTY = 128
PLANE = ("x", "y", "c")
EVERY = ("x", "z", "y", "c")
F32 = jnp.float32
BF16 = jnp.bfloat16
NT = (((1,), (1,)), ((), ()))
TN = (((0,), (0,)), ((), ()))


def whole(a):
    return pl.BlockSpec(a.shape, lambda i: (0,) * len(a.shape), pipeline_mode=pl.Buffered(1))


def call(kernel, out_shape, args, name):
    return pl.pallas_call(
        kernel,
        grid=(1,),
        out_shape=out_shape,
        in_specs=[whole(a) for a in args],
        out_specs=[whole(o) for o in out_shape],
        compiler_params=pltpu.CompilerParams(vmem_limit_bytes=LIMIT),
        cost_estimate=PACKED if name.startswith("pack_far") else COST,
        name=name,
    )(*args)


def sds(shape, dtype):
    return jax.ShapeDtypeStruct(shape, dtype)


def source_kernel(rows_ref, group_ref, member_ref, positive_ref, out_ref):
    rows = rows_ref.shape[0]
    out_ref[:rows, :] = rows_ref[...]
    slot = lax.broadcasted_iota(jnp.int32, group_ref.shape, 0)
    label = jnp.where(slot == 0, jnp.broadcast_to(positive_ref[...], slot.shape), 255)
    for i, part in enumerate((group_ref[...], member_ref[...], label)):
        out_ref[rows:, i * rows : (i + 1) * rows] = part.astype(F32).astype(BF16)


def plan(meta, gid, upper):
    dests, rows = gid.shape
    group, member, label = meta[:, :rows], meta[:, rows : 2 * rows], meta[:, 2 * rows :]
    load = member * 256.0 + label + 1.0
    val = jnp.zeros((dests, rows), F32)
    for s in range(meta.shape[0]):
        val = val + jnp.where(group[s : s + 1, :] == gid, load[s : s + 1, :], 0.0)
    hit = jnp.where(val > 0.0, 1.0, 0.0).astype(BF16)
    rank = jnp.dot(hit, upper, preferred_element_type=F32)
    return val, jnp.where(val > 0.0, rank, -1.0).astype(jnp.int32)


def one_hot(key, each):
    dests, rows = key.shape
    at = lax.broadcasted_iota(jnp.int32, (dests, each, rows), 1)
    hot = jnp.where(jnp.broadcast_to(key[:, None, :], at.shape) == at, 1.0, 0.0)
    return hot.reshape(dests * each, rows).astype(BF16)


def packed(pieces, each, lane0, used, gid_ref, rows_refs, key_ref):
    _, dests, rows = key_ref.shape
    gid = jnp.broadcast_to(gid_ref[:, :1], (dests, rows))
    upper = jnp.where(
        lax.broadcasted_iota(jnp.int32, (rows, rows), 0)
        < lax.broadcasted_iota(jnp.int32, (rows, rows), 1),
        1.0,
        0.0,
    ).astype(BF16)
    lanes = lax.broadcasted_iota(jnp.int32, (dests, 128), 1)
    codes = jnp.zeros((dests, 128), F32)
    total, first = None, 0
    for i, count in enumerate(pieces):
        mine = rows_refs[first : first + count]
        first += count
        size = mine[-1].shape[0]
        val, slot = plan(mine[-1][size - 8 :, :].astype(F32), gid, upper)
        for k in range(CAP):
            found = jnp.sum(jnp.where(slot == k, val, 0.0), axis=1, keepdims=True)
            codes = jnp.where(lanes == lane0 + i * CAP + k, found, codes)
        key = jnp.where(slot >= 0, slot + i * CAP, -1)
        key_ref[i] = key
        hot = one_hot(key, each)
        start = 0
        for r in mine:
            count_rows = min(r.shape[0], rows - start)
            part = jnp.dot(
                hot[:, start : start + count_rows],
                r[:count_rows, :],
                preferred_element_type=F32,
            )
            total = part if total is None else total + part
            start += count_rows
    code = codes.astype(jnp.int32)
    held = (lanes >= lane0) & (lanes < used)
    member = jnp.where(code > 0, (code - 1) >> 8, jnp.where(held, EMPTY, 0)).astype(F32)
    label = jnp.where(code > 0, (code - 1) & 255, 0).astype(F32)
    return total, member, label


def code_rows(member, label, each, row):
    dests = member.shape[0]
    at = lax.broadcasted_iota(jnp.int32, (dests, each, 128), 1)
    return jnp.where(
        at == row,
        jnp.broadcast_to(member[:, None, :], at.shape),
        jnp.where(at == row + 1, jnp.broadcast_to(label[:, None, :], at.shape), 0.0),
    ).reshape(dests * each, 128)


def pack_kernel(pieces, lane0, gid_ref, *refs):
    rows_refs, (out_ref, key_ref) = refs[:-2], refs[-2:]
    total, member, label = packed(pieces, 40, lane0, 128, gid_ref, rows_refs, key_ref)
    extra = code_rows(member, label, 40, 3 * CAP)
    out_ref[:, :128] = (total[:, :128] + extra).astype(BF16)
    out_ref[:, 128:] = total[:, 128:].astype(BF16)


def join_kernel(gid_ref, up_ref, down_ref, tail_ref, out_ref, key_ref):
    dests = gid_ref.shape[0]
    total, member, label = packed((1, 1), 24, 0, 24, gid_ref, (up_ref, down_ref), key_ref)
    extra = code_rows(member, label, 40, 3 * CAP)
    tail = tail_ref[...].astype(F32)
    for lo, hi in ((0, 128), (128, total.shape[1])):
        end = tail[:, lo:hi] + extra if lo == 0 else tail[:, lo:hi]
        both = jnp.concatenate(
            [total[:, lo:hi].reshape(dests, 24, hi - lo), end.reshape(dests, 40, hi - lo)], axis=1
        )
        out_ref[:, lo:hi] = both.reshape(dests * 64, hi - lo).astype(BF16)


def unpacked(key, back_ref, each):
    return lax.dot_general(one_hot(key, each), back_ref[...], TN, preferred_element_type=F32)


def unpack_far_kernel(offset, which, key_ref, back_ref, *outs):
    for i, out in zip(which, outs):
        key = jnp.where(key_ref[i] >= 0, key_ref[i] + offset, -1)
        out[...] = unpacked(key, back_ref, 64).astype(out.dtype)


def unpack_near_kernel(each, key_ref, back_ref, down_ref, up_ref, down_out, up_out):
    down_out[...] = (unpacked(key_ref[1], back_ref, each) + down_ref[...].astype(F32)).astype(BF16)
    up_out[...] = (unpacked(key_ref[2], back_ref, each) + up_ref[...].astype(F32)).astype(BF16)


def unpack_own_kernel(each, key_ref, back_ref, coarse_ref, own_out):
    own_out[...] = unpacked(key_ref[0], back_ref, each) + coarse_ref[...]


def fine_kernel(each, used, per_row, joins, tile, rows_ref, w_ref, *refs):
    if joins:
        ahead_ref, grad_ref, mem_ref, loss_ref, back_ref = refs
    else:
        grad_ref, mem_ref, loss_ref, head_ref, back_ref = refs
    slots = rows_ref.shape[0]
    dests = slots // each
    clusters, labels, features = w_ref.shape
    w = w_ref[...].reshape(clusters * labels, features)
    lane = lax.broadcasted_iota(jnp.int32, (dests, each, 128), 2)
    at = lax.broadcasted_iota(jnp.int32, (dests, each, 128), 1)
    lead = rows_ref[:, :128].astype(F32).reshape(dests, each, 128)

    def column(row):
        flat = jnp.sum(jnp.where(at == row, lead, 0.0), axis=1, keepdims=True)
        spread = jnp.where(lane == at, jnp.broadcast_to(flat, lead.shape), 0.0)
        return jnp.sum(spread, axis=2, keepdims=True).reshape(slots, 1).astype(jnp.int32)

    members, truths = column(used), column(used + 1)
    some = tile // each
    losses = jnp.zeros((1, labels), F32)
    grads, owners = [], []
    for t in range(slots // tile):
        here = slice(t * tile, (t + 1) * tile)
        member_l = jnp.broadcast_to(members[here], (tile, labels))
        truth_id = jnp.broadcast_to(truths[here], (tile, labels))
        all_logits = lax.dot_general(rows_ref[here, :], w, NT, preferred_element_type=F32)
        logits = jnp.zeros((tile, labels), F32)
        for m in range(clusters):
            logits = jnp.where(member_l == m, all_logits[:, m * labels : (m + 1) * labels], logits)
        label = lax.broadcasted_iota(jnp.int32, (tile, labels), 1)
        truth = jnp.where(label == truth_id, 1.0, 0.0)
        bce = jnp.maximum(logits, 0.0) + jnp.log1p(jnp.exp(-jnp.abs(logits))) - truth * logits
        row_loss = jnp.sum(bce, axis=1, keepdims=True) / (per_row * labels)
        losses = losses + jnp.sum(
            jnp.where(label == member_l, jnp.broadcast_to(row_loss, (tile, labels)), 0.0),
            axis=0,
            keepdims=True,
        )
        grad = ((jax.nn.sigmoid(logits) - truth) / per_row).astype(BF16).astype(F32)
        wide = jnp.concatenate(
            [jnp.where(member_l == m, grad, 0.0).astype(BF16) for m in range(clusters)], axis=1
        )
        back = jnp.dot(wide, w, preferred_element_type=F32).reshape(some, each, features)
        if joins:
            ahead = ahead_ref[t * some * 24 : (t + 1) * some * 24, :].astype(F32)
            back = jnp.concatenate([ahead.reshape(some, 24, features), back], axis=1)
            n = some * (each + 24)
            back_ref[t * n : (t + 1) * n, :] = back.reshape(n, features).astype(BF16)
        else:
            n = some * 24
            head_ref[t * n : (t + 1) * n, :] = back[:, :24].reshape(n, features).astype(BF16)
            n = some * (each - 24)
            back_ref[t * n : (t + 1) * n, :] = back[:, 24:].reshape(n, features).astype(BF16)
        grads.append(grad)
        owners.append(member_l.astype(F32))
    grad_ref[...] = jnp.concatenate(grads, axis=0).T.astype(BF16)
    mem_ref[...] = jnp.concatenate(owners, axis=0).T[:8].astype(jnp.int32)

    @pl.when(pl.program_id(0) == 0)
    def _():
        loss_ref[...] = jnp.zeros(loss_ref.shape, F32)

    loss_ref[...] += jnp.broadcast_to(losses, loss_ref.shape)


def fine_part(rows, weight, ahead, each, used, per_row, step, tile, name):
    slots, features = rows.shape
    clusters, labels, _ = weight.shape
    joins = ahead is not None
    sizes = [each + 24] if joins else [24, each - 24]
    dests = step // each
    block = lambda n: pl.BlockSpec((dests * n, features), lambda i: (i, 0))
    return pl.pallas_call(
        lambda *r: fine_kernel(each, used, per_row, joins, tile, *r),
        grid=(slots // step,),
        out_shape=[
            sds((labels, slots), BF16),
            sds((8, slots), jnp.int32),
            sds((8, 128), F32),
            *(sds((slots // each * n, features), BF16) for n in sizes),
        ],
        in_specs=[block(each), whole(weight)] + ([block(24)] if joins else []),
        out_specs=[
            pl.BlockSpec((labels, step), lambda i: (0, i)),
            pl.BlockSpec((8, step), lambda i: (0, i)),
            pl.BlockSpec((8, 128), lambda i: (0, 0)),
            *(block(n) for n in sizes),
        ],
        compiler_params=pltpu.CompilerParams(vmem_limit_bytes=LIMIT),
        cost_estimate=COST,
        name=name,
    )(*((rows, weight, ahead) if joins else (rows, weight)))


def weight_kernel(*refs):
    grads, mems, rows, out_ref = refs[:2], refs[2:4], refs[4:6], refs[6]
    each, labels, features = out_ref.shape
    first = pl.program_id(0) * each
    total = None
    for g_ref, m_ref, r_ref in zip(grads, mems, rows):
        grad = g_ref[...].astype(F32)
        mem = jnp.broadcast_to(m_ref[:1, :], grad.shape)
        wide = jnp.concatenate(
            [jnp.where(mem == first + m, grad, 0.0).astype(BF16) for m in range(each)], axis=0
        )
        part = jnp.dot(wide, r_ref[...], preferred_element_type=F32)
        total = part if total is None else total + part
    out_ref[...] = total.astype(BF16).reshape(out_ref.shape)


def coarse_kernel(target_ref, rows_ref, *refs):
    w_refs, (loss_ref, back_ref) = refs[:-2], refs[-2:]
    rows = rows_ref[...]
    scores = jnp.concatenate(
        [lax.dot_general(rows, w[...], NT, preferred_element_type=F32) for w in w_refs], axis=1
    )
    column = lax.broadcasted_iota(jnp.int32, scores.shape, 1)
    is_target = column == jnp.broadcast_to(target_ref[...], scores.shape)
    top = jnp.max(scores, axis=1, keepdims=True)
    lifted = jnp.exp(scores - top)
    total = jnp.sum(lifted, axis=1, keepdims=True)
    at_target = jnp.sum(jnp.where(is_target, scores, 0.0), axis=1, keepdims=True)
    grad = (lifted * (1.0 / total) - jnp.where(is_target, 1.0, 0.0)).astype(BF16)
    back, start = None, 0
    for w in w_refs:
        part = jnp.dot(grad[:, start : start + w.shape[0]], w[...], preferred_element_type=F32)
        back = part if back is None else back + part
        start += w.shape[0]
    back_ref[...] = back
    loss_ref[...] = top + jnp.log(total) - at_target


def coarse_part(target, rows, weights):
    own, features = rows.shape
    tile = 128
    column = pl.BlockSpec((tile, 1), lambda i: (i, 0))
    block = pl.BlockSpec((tile, features), lambda i: (i, 0))
    return pl.pallas_call(
        coarse_kernel,
        grid=(own // tile,),
        out_shape=[sds((own, 1), F32), sds((own, features), F32)],
        in_specs=[column, block, *(whole(w) for w in weights)],
        out_specs=[column, block],
        compiler_params=pltpu.CompilerParams(vmem_limit_bytes=LIMIT),
        cost_estimate=COST,
        name="coarse",
    )(target[:, None], rows, *weights)


def weight_part(grads, mems, rows, shape):
    clusters, labels, features = shape
    each = 4
    const = lambda a: pl.BlockSpec(a.shape, lambda i: (0, 0), pipeline_mode=pl.Buffered(1))
    args = (*grads, *mems, *rows)
    return pl.pallas_call(
        weight_kernel,
        grid=(clusters // each,),
        out_shape=sds(shape, BF16),
        in_specs=[const(a) for a in args],
        out_specs=pl.BlockSpec((each, labels, features), lambda i: (i, 0, 0)),
        compiler_params=pltpu.CompilerParams(vmem_limit_bytes=LIMIT),
        cost_estimate=COST,
        name="weights",
    )(*args)


def per_device(encoded, coarse_weight, fine_weight, cluster_group, cluster_member, positive):
    own, features = encoded.shape
    clusters, labels, _ = fine_weight.shape
    per_row = cluster_group.shape[1]
    n_z = lax.axis_size("z")
    plane = lax.axis_size(PLANE)
    each_row = lax.axis_size("y") * lax.axis_size("c")
    z = lax.axis_index("z")
    half = own // 2

    def shift(value, by):
        return lax.ppermute(value, "z", [(i, (i + by) % n_z) for i in range(n_z)])

    def exchange(value):
        slots = value.shape[0]
        cube = value.reshape(plane, slots // plane, features)
        return lax.all_to_all(cube, PLANE, 0, 0, tiled=True).reshape(slots, features)

    (source,) = call(
        source_kernel,
        [sds((own + per_row, features), BF16)],
        (encoded, cluster_group.T, cluster_member.T, positive[None, :]),
        "source",
    )
    up1, down1 = shift(source, 1), shift(source, -1)
    up2, down2 = shift(up1, 1), shift(down1, -1)

    def turned(value, axis):
        n = lax.axis_size(axis)
        turns = [
            lax.ppermute(value, axis, [(i, (i - d) % n) for i in range(n)]) for d in range(1, n)
        ]
        return jnp.concatenate([value, *turns], axis=0)

    gathered = lax.optimization_barrier((coarse_weight, source))[0]
    gathered = turned(turned(gathered, "c"), "y")

    dest = jnp.arange(plane, dtype=jnp.int32)
    gid = (dest // each_row) * (each_row * n_z) + z * each_row + dest % each_row
    gid = jnp.broadcast_to(gid[:, None], (plane, 128)).astype(F32)

    keys_of = lambda n: sds((n, plane, own), jnp.int32)

    tail, key_tail = call(
        lambda *r: pack_kernel((1, 1, 1), 24, *r),
        [sds((plane * 40, features), BF16), keys_of(3)],
        (gid, source, up1, down1),
        "pack_tail",
    )
    gathered, tail = lax.optimization_barrier((gathered, tail))
    gathered, tail = lax.optimization_barrier((turned(gathered, "x"), tail))
    near, key_head = call(
        join_kernel,
        [sds((plane * 64, features), BF16), keys_of(2)],
        (gid, up2, down2, tail),
        "pack_near",
    )
    up2, down2, near = lax.optimization_barrier((up2, down2, near))
    up3, down3 = shift(up2, 1), shift(down2, -1)
    far_up, far_down = shift(up3[:half], 1), shift(down3[half:], -1)
    far, key_far = call(
        lambda *r: pack_kernel((1, 1, 2), 0, *r),
        [sds((plane * 40, features), BF16), keys_of(3)],
        (gid, up3, down3, far_up, far_down),
        "pack_far",
    )
    rows_near = exchange(near)

    gathered, far = lax.optimization_barrier((gathered, far))
    weights = [gathered, shift(gathered, 1), shift(gathered, -1)]
    far, rows_near = lax.optimization_barrier((far, rows_near))
    rows_far = exchange(far)
    *weights[1:3], rows_near = lax.optimization_barrier((*weights[1:3], rows_near))
    weights += [shift(weights[1], 1), shift(weights[2], -1)]
    grad_near, mem_near, loss_near, head, back_tail = fine_part(
        rows_near, fine_weight, None, 64, 5 * CAP, per_row, 1024, 256, "fine_near"
    )
    *weights[3:5], head = lax.optimization_barrier((*weights[3:5], head))
    weights += [shift(weights[3], 1), shift(weights[4], -1)]
    grad_far, mem_far, loss_far, back_far = fine_part(
        rows_far, fine_weight, head, 40, 3 * CAP, per_row, 1280, 320, "fine_far"
    )
    *weights[5:7], back_far = lax.optimization_barrier((*weights[5:7], back_far))
    part = gathered.shape[0] // 2
    weights += [shift(weights[5][:part], 1), shift(weights[6][part:], -1)]
    cluster_loss = (loss_near + loss_far)[0, :clusters]

    back_far = exchange(back_far)
    d_fine = weight_part(
        [grad_near, grad_far], [mem_near, mem_far], [rows_near, rows_far], fine_weight.shape
    )
    group = cluster_group[:, 0]
    x, y, c = (lax.axis_index(axis) for axis in PLANE)
    n_x, n_y, n_c = (lax.axis_size(axis) for axis in PLANE)
    from_x = (group // (each_row * n_z) - x) % n_x
    from_y = (group // n_c - y) % n_y
    from_c = (group - c) % n_c
    from_z = (group // each_row - z) % n_z
    at_z = jnp.where(from_z < n_z // 2, 2 * from_z, 2 * (n_z - from_z) - 1)
    place = (((at_z * n_x + from_x) * n_y + from_y) * n_c + from_c) * clusters + cluster_member[:, 0]
    row_loss, coarse_back = coarse_part(place, encoded, weights)
    back_tail, back_far, d_fine, coarse_back = lax.optimization_barrier(
        (back_tail, back_far, d_fine, coarse_back)
    )
    back_tail = exchange(back_tail)
    at_m3, at_3, at_4 = call(
        lambda *r: unpack_far_kernel(24, (0, 1, 2), *r),
        [sds((own, features), F32)] * 2 + [sds((own, features), BF16)],
        (key_far, back_far),
        "unpack_far",
    )
    at_m2, at_2 = call(
        lambda *r: unpack_far_kernel(0, (0, 1), *r),
        [sds((own, features), F32)] * 2,
        (key_head, back_far),
        "unpack_head",
    )
    got_down, got_up = shift(at_4[:half], -1), shift(at_4[half:], 1)
    go_down = at_m3 + jnp.pad(got_down.astype(F32), ((0, half), (0, 0)))
    go_up = at_3 + jnp.pad(got_up.astype(F32), ((half, 0), (0, 0)))
    go_down = at_m2 + shift(go_down.astype(BF16), -1).astype(F32)
    go_up = at_2 + shift(go_up.astype(BF16), 1).astype(F32)
    got_down, got_up = shift(go_down.astype(BF16), -1), shift(go_up.astype(BF16), 1)
    go_down, go_up = call(
        lambda *r: unpack_near_kernel(40, *r),
        [sds((own, features), BF16)] * 2,
        (key_tail, back_tail, got_down, got_up),
        "unpack_near",
    )
    (mine,) = call(
        lambda *r: unpack_own_kernel(40, *r),
        [sds((own, features), F32)],
        (key_tail, back_tail, coarse_back),
        "unpack_own",
    )
    got_down, got_up = shift(go_down, -1).astype(F32), shift(go_up, 1).astype(F32)
    d_encoded = (mine + got_down + got_up).astype(BF16)
    return row_loss[:, 0], d_encoded, d_fine, cluster_loss


def solution(mesh):
    fine_mesh = Mesh(mesh.devices.reshape(4, 8, 4, 2), EVERY)
    rows = P(EVERY)
    wide = P(EVERY, None)
    cube = P(EVERY, None, None)
    return jax.shard_map(
        per_device,
        mesh=fine_mesh,
        in_specs=(wide, wide, cube, wide, wide, rows),
        out_specs=(rows, wide, cube, rows),
        check_vma=False,
    )
```

```python
import jax
import jax.numpy as jnp
from jax import lax
from jax.experimental import pallas as pl
from jax.experimental.pallas import tpu as pltpu
from jax.sharding import Mesh, PartitionSpec as P

CAP = 12
LIMIT = 56 * 2**20
PACKED = pl.CostEstimate(flops=4000000000, bytes_accessed=6 * 10**6, transcendentals=0)
COST = pl.CostEstimate(flops=1, bytes_accessed=1, transcendentals=0)
EMPTY = 128
PLANE = ("x", "y", "c")
EVERY = ("x", "z", "y", "c")
F32 = jnp.float32
BF16 = jnp.bfloat16
NT = (((1,), (1,)), ((), ()))
TN = (((0,), (0,)), ((), ()))


def whole(a):
    return pl.BlockSpec(a.shape, lambda i: (0,) * len(a.shape), pipeline_mode=pl.Buffered(1))


def call(kernel, out_shape, args, name):
    return pl.pallas_call(
        kernel,
        grid=(1,),
        out_shape=out_shape,
        in_specs=[whole(a) for a in args],
        out_specs=[whole(o) for o in out_shape],
        compiler_params=pltpu.CompilerParams(vmem_limit_bytes=LIMIT),
        cost_estimate=PACKED if name.startswith("pack_far") else COST,
        name=name,
    )(*args)


def sds(shape, dtype):
    return jax.ShapeDtypeStruct(shape, dtype)


def source_kernel(rows_ref, group_ref, member_ref, positive_ref, out_ref):
    rows = rows_ref.shape[0]
    out_ref[:rows, :] = rows_ref[...]
    slot = lax.broadcasted_iota(jnp.int32, group_ref.shape, 0)
    label = jnp.where(slot == 0, jnp.broadcast_to(positive_ref[...], slot.shape), 255)
    for i, part in enumerate((group_ref[...], member_ref[...], label)):
        out_ref[rows:, i * rows : (i + 1) * rows] = part.astype(F32).astype(BF16)


def plan(meta, gid, upper):
    dests, rows = gid.shape
    group, member, label = meta[:, :rows], meta[:, rows : 2 * rows], meta[:, 2 * rows :]
    load = member * 256.0 + label + 1.0
    val = jnp.zeros((dests, rows), F32)
    for s in range(meta.shape[0]):
        val = val + jnp.where(group[s : s + 1, :] == gid, load[s : s + 1, :], 0.0)
    hit = jnp.where(val > 0.0, 1.0, 0.0).astype(BF16)
    rank = jnp.dot(hit, upper, preferred_element_type=F32)
    return val, jnp.where(val > 0.0, rank, -1.0).astype(jnp.int32)


def one_hot(key, each):
    dests, rows = key.shape
    at = lax.broadcasted_iota(jnp.int32, (dests, each, rows), 1)
    hot = jnp.where(jnp.broadcast_to(key[:, None, :], at.shape) == at, 1.0, 0.0)
    return hot.reshape(dests * each, rows).astype(BF16)


def packed(pieces, each, lane0, used, gid_ref, rows_refs, key_ref):
    _, dests, rows = key_ref.shape
    gid = jnp.broadcast_to(gid_ref[:, :1], (dests, rows))
    upper = jnp.where(
        lax.broadcasted_iota(jnp.int32, (rows, rows), 0)
        < lax.broadcasted_iota(jnp.int32, (rows, rows), 1),
        1.0,
        0.0,
    ).astype(BF16)
    lanes = lax.broadcasted_iota(jnp.int32, (dests, 128), 1)
    codes = jnp.zeros((dests, 128), F32)
    total, first = None, 0
    for i, count in enumerate(pieces):
        mine = rows_refs[first : first + count]
        first += count
        size = mine[-1].shape[0]
        val, slot = plan(mine[-1][size - 8 :, :].astype(F32), gid, upper)
        for k in range(CAP):
            found = jnp.sum(jnp.where(slot == k, val, 0.0), axis=1, keepdims=True)
            codes = jnp.where(lanes == lane0 + i * CAP + k, found, codes)
        key = jnp.where(slot >= 0, slot + i * CAP, -1)
        key_ref[i] = key
        hot = one_hot(key, each)
        start = 0
        for r in mine:
            count_rows = min(r.shape[0], rows - start)
            part = jnp.dot(
                hot[:, start : start + count_rows],
                r[:count_rows, :],
                preferred_element_type=F32,
            )
            total = part if total is None else total + part
            start += count_rows
    code = codes.astype(jnp.int32)
    held = (lanes >= lane0) & (lanes < used)
    member = jnp.where(code > 0, (code - 1) >> 8, jnp.where(held, EMPTY, 0)).astype(F32)
    label = jnp.where(code > 0, (code - 1) & 255, 0).astype(F32)
    return total, member, label


def code_rows(member, label, each, row):
    dests = member.shape[0]
    at = lax.broadcasted_iota(jnp.int32, (dests, each, 128), 1)
    return jnp.where(
        at == row,
        jnp.broadcast_to(member[:, None, :], at.shape),
        jnp.where(at == row + 1, jnp.broadcast_to(label[:, None, :], at.shape), 0.0),
    ).reshape(dests * each, 128)


def pack_kernel(pieces, lane0, gid_ref, *refs):
    rows_refs, (out_ref, key_ref) = refs[:-2], refs[-2:]
    total, member, label = packed(pieces, 40, lane0, 128, gid_ref, rows_refs, key_ref)
    extra = code_rows(member, label, 40, 3 * CAP)
    out_ref[:, :128] = (total[:, :128] + extra).astype(BF16)
    out_ref[:, 128:] = total[:, 128:].astype(BF16)


def join_kernel(gid_ref, up_ref, down_ref, tail_ref, out_ref, key_ref):
    dests = gid_ref.shape[0]
    total, member, label = packed((1, 1), 24, 0, 24, gid_ref, (up_ref, down_ref), key_ref)
    extra = code_rows(member, label, 40, 3 * CAP)
    tail = tail_ref[...].astype(F32)
    for lo, hi in ((0, 128), (128, total.shape[1])):
        end = tail[:, lo:hi] + extra if lo == 0 else tail[:, lo:hi]
        both = jnp.concatenate(
            [total[:, lo:hi].reshape(dests, 24, hi - lo), end.reshape(dests, 40, hi - lo)], axis=1
        )
        out_ref[:, lo:hi] = both.reshape(dests * 64, hi - lo).astype(BF16)


def unpacked(key, back_ref, each):
    return lax.dot_general(one_hot(key, each), back_ref[...], TN, preferred_element_type=F32)


def unpack_far_kernel(offset, which, key_ref, back_ref, *outs):
    for i, out in zip(which, outs):
        key = jnp.where(key_ref[i] >= 0, key_ref[i] + offset, -1)
        out[...] = unpacked(key, back_ref, 64).astype(out.dtype)


def unpack_near_kernel(each, key_ref, back_ref, down_ref, up_ref, down_out, up_out):
    down_out[...] = (unpacked(key_ref[1], back_ref, each) + down_ref[...].astype(F32)).astype(BF16)
    up_out[...] = (unpacked(key_ref[2], back_ref, each) + up_ref[...].astype(F32)).astype(BF16)


def unpack_own_kernel(each, key_ref, back_ref, coarse_ref, own_out):
    own_out[...] = unpacked(key_ref[0], back_ref, each) + coarse_ref[...]


def fine_kernel(each, used, per_row, joins, tile, rows_ref, w_ref, *refs):
    if joins:
        ahead_ref, grad_ref, mem_ref, loss_ref, back_ref = refs
    else:
        grad_ref, mem_ref, loss_ref, head_ref, back_ref = refs
    slots = rows_ref.shape[0]
    dests = slots // each
    clusters, labels, features = w_ref.shape
    w = w_ref[...].reshape(clusters * labels, features)
    lane = lax.broadcasted_iota(jnp.int32, (dests, each, 128), 2)
    at = lax.broadcasted_iota(jnp.int32, (dests, each, 128), 1)
    lead = rows_ref[:, :128].astype(F32).reshape(dests, each, 128)

    def column(row):
        flat = jnp.sum(jnp.where(at == row, lead, 0.0), axis=1, keepdims=True)
        spread = jnp.where(lane == at, jnp.broadcast_to(flat, lead.shape), 0.0)
        return jnp.sum(spread, axis=2, keepdims=True).reshape(slots, 1).astype(jnp.int32)

    members, truths = column(used), column(used + 1)
    some = tile // each
    losses = jnp.zeros((1, labels), F32)
    grads, owners = [], []
    for t in range(slots // tile):
        here = slice(t * tile, (t + 1) * tile)
        member_l = jnp.broadcast_to(members[here], (tile, labels))
        truth_id = jnp.broadcast_to(truths[here], (tile, labels))
        all_logits = lax.dot_general(rows_ref[here, :], w, NT, preferred_element_type=F32)
        logits = jnp.zeros((tile, labels), F32)
        for m in range(clusters):
            logits = jnp.where(member_l == m, all_logits[:, m * labels : (m + 1) * labels], logits)
        label = lax.broadcasted_iota(jnp.int32, (tile, labels), 1)
        truth = jnp.where(label == truth_id, 1.0, 0.0)
        bce = jnp.maximum(logits, 0.0) + jnp.log1p(jnp.exp(-jnp.abs(logits))) - truth * logits
        row_loss = jnp.sum(bce, axis=1, keepdims=True) / (per_row * labels)
        losses = losses + jnp.sum(
            jnp.where(label == member_l, jnp.broadcast_to(row_loss, (tile, labels)), 0.0),
            axis=0,
            keepdims=True,
        )
        grad = ((jax.nn.sigmoid(logits) - truth) / per_row).astype(BF16).astype(F32)
        wide = jnp.concatenate(
            [jnp.where(member_l == m, grad, 0.0).astype(BF16) for m in range(clusters)], axis=1
        )
        back = jnp.dot(wide, w, preferred_element_type=F32).reshape(some, each, features)
        if joins:
            ahead = ahead_ref[t * some * 24 : (t + 1) * some * 24, :].astype(F32)
            back = jnp.concatenate([ahead.reshape(some, 24, features), back], axis=1)
            n = some * (each + 24)
            back_ref[t * n : (t + 1) * n, :] = back.reshape(n, features).astype(BF16)
        else:
            n = some * 24
            head_ref[t * n : (t + 1) * n, :] = back[:, :24].reshape(n, features).astype(BF16)
            n = some * (each - 24)
            back_ref[t * n : (t + 1) * n, :] = back[:, 24:].reshape(n, features).astype(BF16)
        grads.append(grad)
        owners.append(member_l.astype(F32))
    grad_ref[...] = jnp.concatenate(grads, axis=0).T.astype(BF16)
    mem_ref[...] = jnp.concatenate(owners, axis=0).T[:8].astype(jnp.int32)

    @pl.when(pl.program_id(0) == 0)
    def _():
        loss_ref[...] = jnp.zeros(loss_ref.shape, F32)

    loss_ref[...] += jnp.broadcast_to(losses, loss_ref.shape)


def fine_part(rows, weight, ahead, each, used, per_row, step, tile, name):
    slots, features = rows.shape
    clusters, labels, _ = weight.shape
    joins = ahead is not None
    sizes = [each + 24] if joins else [24, each - 24]
    dests = step // each
    block = lambda n: pl.BlockSpec((dests * n, features), lambda i: (i, 0))
    return pl.pallas_call(
        lambda *r: fine_kernel(each, used, per_row, joins, tile, *r),
        grid=(slots // step,),
        out_shape=[
            sds((labels, slots), BF16),
            sds((8, slots), jnp.int32),
            sds((8, 128), F32),
            *(sds((slots // each * n, features), BF16) for n in sizes),
        ],
        in_specs=[block(each), whole(weight)] + ([block(24)] if joins else []),
        out_specs=[
            pl.BlockSpec((labels, step), lambda i: (0, i)),
            pl.BlockSpec((8, step), lambda i: (0, i)),
            pl.BlockSpec((8, 128), lambda i: (0, 0)),
            *(block(n) for n in sizes),
        ],
        compiler_params=pltpu.CompilerParams(vmem_limit_bytes=LIMIT),
        cost_estimate=COST,
        name=name,
    )(*((rows, weight, ahead) if joins else (rows, weight)))


def weight_kernel(*refs):
    grads, mems, rows, out_ref = refs[:2], refs[2:4], refs[4:6], refs[6]
    each, labels, features = out_ref.shape
    first = pl.program_id(0) * each
    total = None
    for g_ref, m_ref, r_ref in zip(grads, mems, rows):
        grad = g_ref[...].astype(F32)
        mem = jnp.broadcast_to(m_ref[:1, :], grad.shape)
        wide = jnp.concatenate(
            [jnp.where(mem == first + m, grad, 0.0).astype(BF16) for m in range(each)], axis=0
        )
        part = jnp.dot(wide, r_ref[...], preferred_element_type=F32)
        total = part if total is None else total + part
    out_ref[...] = total.astype(BF16).reshape(out_ref.shape)


def coarse_kernel(target_ref, rows_ref, *refs):
    w_refs, (loss_ref, back_ref) = refs[:-2], refs[-2:]
    rows = rows_ref[...]
    scores = jnp.concatenate(
        [lax.dot_general(rows, w[...], NT, preferred_element_type=F32) for w in w_refs], axis=1
    )
    column = lax.broadcasted_iota(jnp.int32, scores.shape, 1)
    is_target = column == jnp.broadcast_to(target_ref[...], scores.shape)
    top = jnp.max(scores, axis=1, keepdims=True)
    lifted = jnp.exp(scores - top)
    total = jnp.sum(lifted, axis=1, keepdims=True)
    at_target = jnp.sum(jnp.where(is_target, scores, 0.0), axis=1, keepdims=True)
    grad = (lifted * (1.0 / total) - jnp.where(is_target, 1.0, 0.0)).astype(BF16)
    back, start = None, 0
    for w in w_refs:
        part = jnp.dot(grad[:, start : start + w.shape[0]], w[...], preferred_element_type=F32)
        back = part if back is None else back + part
        start += w.shape[0]
    back_ref[...] = back
    loss_ref[...] = top + jnp.log(total) - at_target


def coarse_part(target, rows, weights):
    own, features = rows.shape
    tile = 128
    column = pl.BlockSpec((tile, 1), lambda i: (i, 0))
    block = pl.BlockSpec((tile, features), lambda i: (i, 0))
    return pl.pallas_call(
        coarse_kernel,
        grid=(own // tile,),
        out_shape=[sds((own, 1), F32), sds((own, features), F32)],
        in_specs=[column, block, *(whole(w) for w in weights)],
        out_specs=[column, block],
        compiler_params=pltpu.CompilerParams(vmem_limit_bytes=LIMIT),
        cost_estimate=COST,
        name="coarse",
    )(target[:, None], rows, *weights)


def weight_part(grads, mems, rows, shape):
    clusters, labels, features = shape
    each = 4
    const = lambda a: pl.BlockSpec(a.shape, lambda i: (0, 0), pipeline_mode=pl.Buffered(1))
    args = (*grads, *mems, *rows)
    return pl.pallas_call(
        weight_kernel,
        grid=(clusters // each,),
        out_shape=sds(shape, BF16),
        in_specs=[const(a) for a in args],
        out_specs=pl.BlockSpec((each, labels, features), lambda i: (i, 0, 0)),
        compiler_params=pltpu.CompilerParams(vmem_limit_bytes=LIMIT),
        cost_estimate=COST,
        name="weights",
    )(*args)


def per_device(encoded, coarse_weight, fine_weight, cluster_group, cluster_member, positive):
    own, features = encoded.shape
    clusters, labels, _ = fine_weight.shape
    per_row = cluster_group.shape[1]
    n_z = lax.axis_size("z")
    plane = lax.axis_size(PLANE)
    each_row = lax.axis_size("y") * lax.axis_size("c")
    z = lax.axis_index("z")
    half = own // 2

    def shift(value, by):
        return lax.ppermute(value, "z", [(i, (i + by) % n_z) for i in range(n_z)])

    def exchange(value):
        slots = value.shape[0]
        cube = value.reshape(plane, slots // plane, features)
        return lax.all_to_all(cube, PLANE, 0, 0, tiled=True).reshape(slots, features)

    (source,) = call(
        source_kernel,
        [sds((own + per_row, features), BF16)],
        (encoded, cluster_group.T, cluster_member.T, positive[None, :]),
        "source",
    )
    up1, down1 = shift(source, 1), shift(source, -1)
    up2, down2 = shift(up1, 1), shift(down1, -1)

    def turned(value, axis):
        n = lax.axis_size(axis)
        turns = [
            lax.ppermute(value, axis, [(i, (i - d) % n) for i in range(n)]) for d in range(1, n)
        ]
        return jnp.concatenate([value, *turns], axis=0)

    gathered = turned(turned(coarse_weight, "c"), "y")

    dest = jnp.arange(plane, dtype=jnp.int32)
    gid = (dest // each_row) * (each_row * n_z) + z * each_row + dest % each_row
    gid = jnp.broadcast_to(gid[:, None], (plane, 128)).astype(F32)

    keys_of = lambda n: sds((n, plane, own), jnp.int32)

    tail, key_tail = call(
        lambda *r: pack_kernel((1, 1, 1), 24, *r),
        [sds((plane * 40, features), BF16), keys_of(3)],
        (gid, source, up1, down1),
        "pack_tail",
    )
    gathered, tail = lax.optimization_barrier((turned(gathered, "x"), tail))
    near, key_head = call(
        join_kernel,
        [sds((plane * 64, features), BF16), keys_of(2)],
        (gid, up2, down2, tail),
        "pack_near",
    )
    up2, down2, near = lax.optimization_barrier((up2, down2, near))
    up3, down3 = shift(up2, 1), shift(down2, -1)
    far_up, far_down = shift(up3[:half], 1), shift(down3[half:], -1)
    far, key_far = call(
        lambda *r: pack_kernel((1, 1, 2), 0, *r),
        [sds((plane * 40, features), BF16), keys_of(3)],
        (gid, up3, down3, far_up, far_down),
        "pack_far",
    )
    rows_near = exchange(near)

    gathered, far = lax.optimization_barrier((gathered, far))
    weights = [gathered, shift(gathered, 1), shift(gathered, -1)]
    far, rows_near = lax.optimization_barrier((far, rows_near))
    rows_far = exchange(far)
    *weights[1:3], rows_near = lax.optimization_barrier((*weights[1:3], rows_near))
    weights += [shift(weights[1], 1), shift(weights[2], -1)]
    grad_near, mem_near, loss_near, head, back_tail = fine_part(
        rows_near, fine_weight, None, 64, 5 * CAP, per_row, 1024, 256, "fine_near"
    )
    *weights[3:5], head = lax.optimization_barrier((*weights[3:5], head))
    weights += [shift(weights[3], 1), shift(weights[4], -1)]
    grad_far, mem_far, loss_far, back_far = fine_part(
        rows_far, fine_weight, head, 40, 3 * CAP, per_row, 640, 320, "fine_far"
    )
    *weights[5:7], back_far = lax.optimization_barrier((*weights[5:7], back_far))
    weights.append(shift(weights[5], 1))
    cluster_loss = (loss_near + loss_far)[0, :clusters]

    back_far = exchange(back_far)
    d_fine = weight_part(
        [grad_near, grad_far], [mem_near, mem_far], [rows_near, rows_far], fine_weight.shape
    )
    group = cluster_group[:, 0]
    x, y, c = (lax.axis_index(axis) for axis in PLANE)
    n_x, n_y, n_c = (lax.axis_size(axis) for axis in PLANE)
    from_x = (group // (each_row * n_z) - x) % n_x
    from_y = (group // n_c - y) % n_y
    from_c = (group - c) % n_c
    from_z = (group // each_row - z) % n_z
    at_z = jnp.where(from_z < n_z // 2, 2 * from_z, 2 * (n_z - from_z) - 1)
    place = (((at_z * n_x + from_x) * n_y + from_y) * n_c + from_c) * clusters + cluster_member[:, 0]
    row_loss, coarse_back = coarse_part(place, encoded, weights)
    back_tail, back_far, d_fine, coarse_back = lax.optimization_barrier(
        (back_tail, back_far, d_fine, coarse_back)
    )
    back_tail = exchange(back_tail)
    at_m3, at_3, at_4 = call(
        lambda *r: unpack_far_kernel(24, (0, 1, 2), *r),
        [sds((own, features), F32)] * 2 + [sds((own, features), BF16)],
        (key_far, back_far),
        "unpack_far",
    )
    at_m2, at_2 = call(
        lambda *r: unpack_far_kernel(0, (0, 1), *r),
        [sds((own, features), F32)] * 2,
        (key_head, back_far),
        "unpack_head",
    )
    got_down, got_up = shift(at_4[:half], -1), shift(at_4[half:], 1)
    go_down = at_m3 + jnp.pad(got_down.astype(F32), ((0, half), (0, 0)))
    go_up = at_3 + jnp.pad(got_up.astype(F32), ((half, 0), (0, 0)))
    go_down = at_m2 + shift(go_down.astype(BF16), -1).astype(F32)
    go_up = at_2 + shift(go_up.astype(BF16), 1).astype(F32)
    got_down, got_up = shift(go_down.astype(BF16), -1), shift(go_up.astype(BF16), 1)
    go_down, go_up = call(
        lambda *r: unpack_near_kernel(40, *r),
        [sds((own, features), BF16)] * 2,
        (key_tail, back_tail, got_down, got_up),
        "unpack_near",
    )
    (mine,) = call(
        lambda *r: unpack_own_kernel(40, *r),
        [sds((own, features), F32)],
        (key_tail, back_tail, coarse_back),
        "unpack_own",
    )
    got_down, got_up = shift(go_down, -1).astype(F32), shift(go_up, 1).astype(F32)
    d_encoded = (mine + got_down + got_up).astype(BF16)
    return row_loss[:, 0], d_encoded, d_fine, cluster_loss


def solution(mesh):
    fine_mesh = Mesh(mesh.devices.reshape(4, 8, 4, 2), EVERY)
    rows = P(EVERY)
    wide = P(EVERY, None)
    cube = P(EVERY, None, None)
    return jax.shard_map(
        per_device,
        mesh=fine_mesh,
        in_specs=(wide, wide, cube, wide, wide, rows),
        out_specs=(rows, wide, cube, rows),
        check_vma=False,
    )
```
